256 devices in a mesh: row: 16 (over y, z_lo, core), col: 16 (over z_hi, x).
Axes of the slice: x: 4, y: 4, z: 8 (z_hi: 4, z_lo: 2; z = z_hi * 2 + z_lo), core: 2. Of those that a mesh axis runs over, the one named last changes fastest.
Arguments:
- tokens: bfloat16 [4096, 8192], P('col', 'row'), may hold values from -6 to 6
- grad_out: bfloat16 [4096, 16384], P('row', 'col'), may hold values from -6 to 6
- base_weight: float32 [8192, 16384], P('row', 'col'), may hold values from -6 to 6
- left_param: float32 [16, 512, 512], P('row'), may hold values from -6 to 6
- right_param: float32 [64, 256, 256], P('col'), may hold values from -6 to 6
Outputs:
- rotated_weight: float32 [8192, 16384], P('row', 'col')
- new_left: float32 [16, 512, 512], P('row')
- new_right: float32 [64, 256, 256], P('col')
The draws below stay inside these ranges and needn't reach their ends.
All inputs are finite; a program needn't handle non-finite values.
Results may differ from the reference program's by a relative error of at most 0.0003.
Values may be sent and summed in bfloat16 or wider, within the bound.
A program may use at most 128 MiB of HBM per device.

```python
import math
import jax
import jax.numpy as jnp
from jax import lax

D = 8192
FF = 16384
LBLK = 512
RBLK = 256
TOKENS = 4096


def level_of(key, extent, split, least, largest):
    def one(position, blocks):
        draws = jax.random.uniform(jax.random.fold_in(jax.random.fold_in(key, 6), position), (blocks,), jnp.float32, least / len(split), largest / len(split))
        return jnp.repeat(jnp.exp(draws), extent[position] // blocks).reshape((-1,) + (1,) * (len(extent) - position - 1))

    gain = one(*split[0])
    for cut in split[1:]:
        gain = gain * one(*cut)
    return gain


def centred(rng, dims, scale, most, pieces=(), kind=jnp.bfloat16):
    result = jax.random.normal(rng, dims, jnp.float32) * scale
    if len(pieces) > 0:
        result = level_of(rng, dims, pieces, -0.22, 0.18) * result
    return jnp.clip(result, min=-most, max=most).astype(kind)


def setup_inputs(seed: int = 0) -> dict:
    key_list = jax.random.split(jax.random.key(seed), 6)
    tokens = centred(key_list[0], (TOKENS, D), 1.0, 6.0, ((0, 16), (1, 16)))
    grad_out = centred(key_list[1], (TOKENS, FF), 1.0, 6.0, ((0, 16), (1, 16)))
    base_weight = centred(key_list[2], (D, FF), 1.0, 6.0, ((0, 16), (1, 16)), jnp.float32)
    left_param = centred(key_list[3], (D // LBLK, LBLK, LBLK), 1.0, 6.0, ((0, 16),), jnp.float32)
    right_param = centred(key_list[4], (FF // RBLK, RBLK, RBLK), 1.0, 6.0, ((0, 16),), jnp.float32)
    return {"tokens": tokens, "grad_out": grad_out, "base_weight": base_weight, "left_param": left_param, "right_param": right_param}


precise = lax.Precision.HIGHEST
taylor_degree = 6
step_rate = 0.3
epsilon = 1e-06

def batch_product(first, second):
    return jnp.einsum('lab,lbc->lac', first, second, precision=precise)

def transpose_last(matrix):
    return jnp.swapaxes(matrix, 1, 2)

def skew_from(param):
    skew_scale = 0.5 / math.sqrt(param.shape[-1])
    return skew_scale * (param - transpose_last(param))

def column_levels(skew, col_start, col_width):
    dimension = skew.shape[-1]
    eye_part = (jnp.arange(dimension)[:, None] == col_start + jnp.arange(col_width)[None, :]).astype(jnp.float32)
    current = eye_part[None] + lax.dynamic_slice_in_dim(skew, col_start, col_width, 2) / taylor_degree
    horner_levels = [current] * (taylor_degree + 1)
    for divisor in range(taylor_degree - 1, 0, -1):
        current = eye_part[None] + batch_product(skew, current) / divisor
        horner_levels[divisor] = current
    return horner_levels

def adjoint(skew, horner_levels, upper_grad):
    running = jnp.zeros(skew.shape, jnp.float32)
    for divisor in range(1, taylor_degree):
        running = running + batch_product(upper_grad, transpose_last(horner_levels[divisor + 1])) / divisor
        upper_grad = batch_product(transpose_last(skew), upper_grad) / divisor
    return (running, upper_grad)

def update_param(param, accum):
    skew_scale = 0.5 / math.sqrt(param.shape[-1])
    grad_param = skew_scale * (accum - transpose_last(accum))
    root_mean = jnp.sqrt(lax.optimization_barrier(jnp.mean(grad_param * grad_param, axis=(1, 2), keepdims=True)) + epsilon)
    return param - step_rate * grad_param / root_mean

def right_apply(weight, rotation):
    count = rotation.shape[0]
    block = rotation.shape[-1]
    shaped = weight.reshape(weight.shape[0], count, block)
    return jnp.einsum('nbr,brs->nbs', shaped, rotation, precision=precise).reshape(weight.shape)

def reference(tokens, grad_out, base_weight, left_param, right_param):
    left_skew = skew_from(left_param)
    right_skew = skew_from(right_param)
    left_levels = column_levels(left_skew, 0, LBLK)
    right_levels = column_levels(right_skew, 0, RBLK)
    left_rot = left_levels[1]
    right_rot = right_levels[1]
    left_count = D // LBLK
    right_count = FF // RBLK

    def per_block(carried, block_index):
        weight = lax.dynamic_slice_in_dim(base_weight, block_index * LBLK, LBLK, 0)
        token_rows = lax.dynamic_slice_in_dim(tokens, block_index * LBLK, LBLK, 1)
        rotation = lax.dynamic_index_in_dim(left_rot, block_index, 0, keepdims=False)
        grad_weight = jnp.dot(token_rows.T, grad_out, preferred_element_type=jnp.float32)
        mixed_weight = right_apply(weight, right_rot)
        left_part = jnp.dot(grad_weight, mixed_weight.T, precision=precise)
        rotated = jnp.dot(rotation, weight, precision=precise)
        right_part = jnp.einsum('nbr,nbs->brs', rotated.reshape(LBLK, right_count, RBLK), grad_weight.reshape(LBLK, right_count, RBLK), precision=precise)
        return (carried + right_part, left_part)
    start_right = jnp.zeros((right_count, RBLK, RBLK), jnp.float32)
    right_grad, left_grad = lax.scan(per_block, start_right, jnp.arange(left_count, dtype=jnp.int32))
    left_acc, left_upper = adjoint(left_skew, left_levels, left_grad)
    left_acc = left_acc + left_upper / taylor_degree
    right_acc, right_upper = adjoint(right_skew, right_levels, right_grad)
    right_acc = right_acc + right_upper / taylor_degree
    new_left = update_param(left_param, left_acc)
    new_right = update_param(right_param, right_acc)
    new_left_rot = column_levels(skew_from(new_left), 0, LBLK)[1]
    new_right_rot = column_levels(skew_from(new_right), 0, RBLK)[1]

    def rotate_block(carried, block_index):
        weight = lax.dynamic_slice_in_dim(base_weight, block_index * LBLK, LBLK, 0)
        rotation = lax.dynamic_index_in_dim(new_left_rot, block_index, 0, keepdims=False)
        turned = jnp.dot(rotation, weight, precision=precise)
        return (carried, right_apply(turned, new_right_rot))
    unused, turned_blocks = lax.scan(rotate_block, jnp.zeros((), jnp.float32), jnp.arange(left_count, dtype=jnp.int32))
    rotated_weight = turned_blocks.reshape(D, FF)
    return (rotated_weight, new_left, new_right)
```

```python
import math

import jax
import jax.numpy as jnp
from jax import lax
from jax.experimental import pallas as pl
from jax.experimental.pallas import tpu as pltpu
from jax.sharding import PartitionSpec as P

step_rate = 0.3
epsilon = 1e-06
f32 = jnp.float32
bf16 = jnp.bfloat16
C2, C3, C4, C5, C6 = 1 / 2, 1 / 6, 1 / 24, 1 / 120, 1 / 720
LB, RB = 512, 256
NN = (((1,), (0,)), ((), ()))
NT = (((1,), (1,)), ((), ()))


def split(value):
    high = value.astype(bf16)
    return high, (value - high.astype(f32)).astype(bf16)


def put(pair, value, where=Ellipsis):
    pair[0][where], pair[1][where] = split(value)


def dot(first, second, dims=NN):
    return lax.dot_general(first, second, dims, preferred_element_type=f32)


def dot3(first, second, dims=NN):
    ah, al = first
    bh, bl = second
    return dot(ah, bh, dims) + (dot(ah, bl, dims) + dot(al, bh, dims))


def get(pair, where=Ellipsis):
    return pair[0][where], pair[1][where]


def rows_loop(total, tile, fn):
    def step(index, carry):
        fn(pl.ds(pl.multiple_of(index * tile, tile), tile))
        return carry

    lax.fori_loop(0, total // tile, step, 0)


def eye(rows, size):
    r = lax.broadcasted_iota(jnp.int32, (rows.size, size), 0) + rows.start
    c = lax.broadcasted_iota(jnp.int32, (rows.size, size), 1)
    return jnp.where(r == c, 1.0, 0.0).astype(f32)


def poly(size, tile, S, SP, AP, BP, CP, Af, finish, CT=None):
    def square(rows):
        a = dot3(get(SP, rows), get(SP))
        Af[rows] = a
        put(AP, a, rows)

    rows_loop(size, tile, square)

    def cube(rows):
        b = dot3(get(SP, rows), get(AP))
        put(BP, b, rows)
        s = S[rows]
        a = Af[rows]
        even = C3 * eye(rows, size) + C5 * a
        odd = C4 * s + C6 * b
        put(CP, even + odd, rows)
        if CT is not None:
            put(CT, even - odd, rows)

    rows_loop(size, tile, cube)

    def last(rows):
        finish(rows, eye(rows, size) + S[rows] + C2 * Af[rows] + dot3(get(BP, rows), get(CP)))

    rows_loop(size, tile, last)


def adjoint(size, tile, G, GP, SP, AP, BP, CT, EP, Ea, Aa, Eb):
    put(GP, G[...])

    def first(rows):
        c_bar = -dot3(get(BP, rows), get(GP))
        b_bar = dot3(get(GP, rows), get(CT)) + C6 * c_bar
        put(EP, b_bar, rows)
        g = G[rows]
        Ea[rows] = g + C4 * c_bar
        Aa[rows] = C2 * g + C5 * c_bar

    rows_loop(size, tile, first)

    def second(rows):
        Ea[rows] += dot3(get(EP, rows), get(AP))
        Aa[rows] -= dot3(get(SP, rows), get(EP))

    rows_loop(size, tile, second)
    a_bar = Aa[...]
    put(GP, a_bar + a_bar.T)

    def third(rows):
        Eb[rows] = Ea[rows] - dot3(get(GP, rows), get(SP))

    rows_loop(size, tile, third)
    e = Eb[...]
    return e - e.T


def updated(param, diff, size):
    p = (0.5 / math.sqrt(size)) * diff
    mean = jnp.sum(p * p) * (1.0 / (size * size))
    return param - step_rate * p / jnp.sqrt(mean + epsilon)


def comm_kernel(
    tok_ref, grad_ref, w_ref, lp_ref, rp_ref, nl_ref, nr_ref,
    T, Gr, gw, gwh, gwl, mh, ml, qh, ql, lw,
    lS, lA, lsh, lsl, lah, lal, lbh, lbl, lch, lcl, lth, ltl, lrh, lrl, lgh, lgl,
    rS, rA, rsh, rsl, rah, ral, rbh, rbl, rch, rcl, rth, rtl, rrh, rrl,
    lpart, xr, xs, Q, zr, zs, Fx,
    rpart, rc, rq, yr, ys, ro, rz, Fy,
    t_recv, t_send, g_recv, g_send, loc_sem,
    xr_sem, zr_sem, za_sem, xa_sem, l_send,
    rc_sem, yr_sem, rz_sem, ya_sem, ra_sem, r_send,
):
    row = lax.axis_index("row")
    col = lax.axis_index("col")
    y, z, c = row // 4, (row // 2) % 2, row % 2
    h, x = col // 4, col % 4

    def row_of(yy, zz, cc):
        return (lax.rem(yy + 4, 4) * 2 + zz) * 2 + cc

    def col_of(hh, xx):
        return lax.rem(hh + 4, 4) * 4 + lax.rem(xx + 4, 4)

    YP, YM = {"row": row_of(y + 1, z, c)}, {"row": row_of(y + 3, z, c)}
    ZZ, CC = {"row": row_of(y, 1 - z, c)}, {"row": row_of(y, z, 1 - c)}
    XP, XM = {"col": col_of(h, x + 1)}, {"col": col_of(h, x + 3)}
    HP, HM = {"col": col_of(h + 1, x)}, {"col": col_of(h + 3, x)}
    started = []

    def send(src, dst, sems, recv, dev):
        counter = sems[1]
        copy = pltpu.make_async_remote_copy(
            src_ref=src, dst_ref=dst, send_sem=sems[0].at[counter[0]], recv_sem=recv,
            device_id=dev, device_id_type=pl.DeviceIdType.MESH,
        )
        counter[0] += 1
        copy.start()
        started.append(copy)

    def arrive(dst, recv):
        pltpu.make_async_remote_copy(
            src_ref=dst, dst_ref=dst, send_sem=loc_sem.at[2], recv_sem=recv,
            device_id=CC, device_id_type=pl.DeviceIdType.MESH,
        ).wait_recv()

    ts, gs, ls, rs = (t_send, [0]), (g_send, [0]), (l_send, [0]), (r_send, [0])

    barrier = pltpu.get_barrier_semaphore()
    for dev in (YP, YM, ZZ, CC, XP, XM, HP, HM):
        pl.semaphore_signal(barrier, inc=1, device_id=dev, device_id_type=pl.DeviceIdType.MESH)
    pl.semaphore_wait(barrier, 8)

    def t_half(ref, half):
        return ref.at[pl.ds(256 * half, 256)]

    def g_half(ref, half):
        return ref.at[pl.ds(128 * half, 128)]

    def t_go(shard, half, dev, own=False):
        src = t_half(tok_ref if own else T.at[shard], half)
        send(src, t_half(T.at[shard], half), ts, t_recv.at[shard, half], dev)

    def t_in(shard, half):
        arrive(t_half(T.at[shard], half), t_recv.at[shard, half])

    def g_go(shard, half, dev, own=False):
        src = g_half(grad_ref if own else Gr.at[shard], half)
        send(src, g_half(Gr.at[shard], half), gs, g_recv.at[shard, half], dev)

    def g_in(shard, half):
        arrive(g_half(Gr.at[shard], half), g_recv.at[shard, half])

    for half in (0, 1):
        t_go(col, half, XP, True)
        t_go(col, 1 - half, XM, True)
        t_go(col, half, HP, True)
        t_go(col, 1 - half, HM, True)
        g_go(row, half, YP, True)
        g_go(row, 1 - half, YM, True)
    for half in (0, 1):
        g_go(row, half, ZZ, True)
        g_go(row, half, CC, True)
    local_t = pltpu.make_async_copy(tok_ref, T.at[col], loc_sem.at[0])
    local_g = pltpu.make_async_copy(grad_ref, Gr.at[row], loc_sem.at[1])
    local_t.start()
    local_g.start()

    def t_ring(hh):
        a, b = col_of(hh, x + 3), col_of(hh, x + 1)
        t_in(a, 0)
        t_go(a, 0, XP)
        t_in(b, 1)
        t_go(b, 1, XM)

    def t_rest(hh):
        t_in(col_of(hh, x + 3), 1)
        t_in(col_of(hh, x + 1), 0)
        t_in(col_of(hh, x + 2), 0)
        t_in(col_of(hh, x + 2), 1)

    def t_spread(shard):
        t_go(shard, 0, XP)
        t_go(shard, 1, XM)
        t_go(shard, 1, XP)
        t_go(shard, 0, XM)

    def g_ring(zz):
        a, b = row_of(y + 3, zz, c), row_of(y + 1, zz, c)
        g_in(a, 0)
        g_go(a, 0, YP)
        g_go(a, 0, CC)
        g_in(b, 1)
        g_go(b, 1, YM)
        g_go(b, 1, CC)

    def g_rest(zz):
        a, b = row_of(y + 3, zz, c), row_of(y + 1, zz, c)
        g_in(a, 1)
        g_go(a, 1, CC)
        g_in(b, 0)
        g_go(b, 0, CC)

    def g_far(zz):
        far = row_of(y + 2, zz, c)
        for half in (0, 1):
            g_in(far, half)
            g_go(far, half, CC)

    lSP, lAP, lBP, lCP, lCT = (lsh, lsl), (lah, lal), (lbh, lbl), (lch, lcl), (lth, ltl)
    lRP, lGP = (lrh, lrl), (lgh, lgl)
    MP, QP, GWP = (mh, ml), (qh, ql), (gwh, gwl)

    def at(pair, index):
        return tuple(ref.at[index] for ref in pair)

    rSP, rAP, rBP, rCP, rCT = (rsh, rsl), (rah, ral), (rbh, rbl), (rch, rcl), (rth, rtl)
    rRP = (rrh, rrl)


    def right_one(index, carry):
        param = rp_ref[index]
        s = (0.5 / math.sqrt(RB)) * (param - param.T)
        rS[index] = s
        put(at(rSP, index), s)
        poly(
            RB, RB, rS.at[index], at(rSP, index), at(rAP, index), at(rBP, index), at(rCP, index), rA.at[index],
            lambda rows, value: put(at(rRP, index), value, rows), at(rCT, index),
        )
        return carry

    lax.fori_loop(0, 1, right_one, 0)
    t_ring(h)
    lax.fori_loop(1, 2, right_one, 0)
    g_ring(z)
    lax.fori_loop(2, 4, right_one, 0)

    t_in(col_of(h + 3, x), 0)
    t_go(col_of(h + 3, x), 0, HP)
    t_in(col_of(h + 1, x), 1)
    t_go(col_of(h + 1, x), 1, HM)
    t_in(col_of(h + 3, x), 1)
    t_spread(col_of(h + 3, x))
    t_in(col_of(h + 1, x), 0)
    t_spread(col_of(h + 1, x))

    param = lp_ref[...]
    s = (0.5 / math.sqrt(LB)) * (param - param.T)
    lS[...] = s
    put(lSP, s)

    other = row_of(y, 1 - z, c)
    for half in (0, 1):
        g_in(other, half)
    g_go(other, 0, YP)
    g_go(other, 1, YM)
    g_go(other, 1, YP)
    g_go(other, 0, YM)
    g_go(other, 0, CC)
    g_go(other, 1, CC)
    g_rest(z)

    def weight_right(rows):
        for index in range(4):
            cols = slice(RB * index, RB * (index + 1))
            m = dot3(split(w_ref[rows, cols]), get(at(rRP, index)))
            mh[rows, cols], ml[rows, cols] = split(m)

    rows_loop(LB, 256, weight_right)
    t_ring(h + 3)
    t_ring(h + 1)
    g_far(z)

    poly(LB, 256, lS, lSP, lAP, lBP, lCP, lA, lambda rows, value: put(lRP, value, rows), lCT)

    t_in(col_of(h + 2, x), 0)
    t_in(col_of(h + 2, x), 1)
    t_spread(col_of(h + 2, x))
    g_ring(1 - z)

    def left_weight(index, carry):
        cols = pl.ds(pl.multiple_of(index * 256, 256), 256)
        lw = dot3(get(lRP), split(w_ref[:, cols]))
        put(QP, lw.T, cols)
        return carry

    lax.fori_loop(0, 4, left_weight, 0)

    t_rest(h)
    t_ring(h + 2)
    t_rest(h + 3)
    t_rest(h + 1)
    g_rest(1 - z)

    local_t.wait()
    local_g.wait()

    def add_chunks(pieces, start):
        def go(rows):
            total = None
            for k in pieces:
                part = dot(T[k, rows], Gr[k])
                total = part if total is None else total + part
            if start:
                gw[rows] = total
            else:
                gw[rows] += total

        rows_loop(LB, 256, go)

    t_rest(h + 2)

    def partner(yy, zz):
        far = row_of(yy, zz, 1 - c)
        g_in(far, 0)
        g_in(far, 1)
        return [row_of(yy, zz, c), far]

    add_chunks(partner(y, z) + partner(y + 3, z), True)
    add_chunks(partner(y + 1, z) + partner(y + 2, z), False)
    add_chunks(partner(y, 1 - z) + partner(y + 3, 1 - z), False)
    g_far(1 - z)
    add_chunks(partner(y + 1, 1 - z) + partner(y + 2, 1 - z), False)

    put(GWP, gw[...])

    def left_partial(index, carry):
        rows = pl.ds(pl.multiple_of(index * 128, 128), 128)
        lpart[index] = dot3(get(GWP, rows), get(MP), NT).reshape(2, 64, LB)
        return carry

    lax.fori_loop(0, 4, left_partial, 0)

    def rs_open(part, me, buf, sem, snd, plus, minus):
        far, nxt, prv = lax.rem(me + 2, 4), lax.rem(me + 1, 4), lax.rem(me + 3, 4)
        send(part(far, 0), buf.at[0], snd, sem.at[0], plus)
        send(part(far, 1), buf.at[1], snd, sem.at[1], minus)
        send(part(nxt, 1), buf.at[2], snd, sem.at[2], plus)
        send(part(prv, 0), buf.at[3], snd, sem.at[3], minus)

    def rs_mid(part, me, buf, stage, sem, snd, plus, minus):
        nxt, prv = lax.rem(me + 1, 4), lax.rem(me + 3, 4)
        arrive(buf.at[0], sem.at[0])
        stage[0] = buf[0] + part(nxt, 0)[...]
        arrive(buf.at[1], sem.at[1])
        stage[1] = buf[1] + part(prv, 1)[...]
        send(stage.at[0], buf.at[4], snd, sem.at[4], plus)
        send(stage.at[1], buf.at[5], snd, sem.at[5], minus)

    def rs_close(part, me, buf, sem):
        for index in range(2, 6):
            arrive(buf.at[index], sem.at[index])
        first = part(me, 0)[...] + (buf[3] + buf[4])
        second = part(me, 1)[...] + (buf[2] + buf[5])
        return first, second

    def ag_open(piece, me, sem, snd, plus, minus):
        for half in (0, 1):
            send(piece(me, half), piece(me, half), snd, sem.at[me, half], plus)
            send(piece(me, 1 - half), piece(me, 1 - half), snd, sem.at[me, 1 - half], minus)

    def ag_mid(piece, me, sem, snd, plus, minus):
        nxt, prv = lax.rem(me + 1, 4), lax.rem(me + 3, 4)
        arrive(piece(prv, 0), sem.at[prv, 0])
        send(piece(prv, 0), piece(prv, 0), snd, sem.at[prv, 0], plus)
        arrive(piece(nxt, 1), sem.at[nxt, 1])
        send(piece(nxt, 1), piece(nxt, 1), snd, sem.at[nxt, 1], minus)

    def ag_close(piece, me, sem):
        far, nxt, prv = lax.rem(me + 2, 4), lax.rem(me + 1, 4), lax.rem(me + 3, 4)
        for who, half in ((prv, 1), (nxt, 0), (far, 0), (far, 1)):
            arrive(piece(who, half), sem.at[who, half])

    def l_part(chunk, half):
        return lpart.at[chunk, half]

    def q_part(chunk, half):
        return Q.at[chunk, half]

    def z_piece(chunk, half):
        return Fx.at[x, chunk, half]

    def x_piece(chunk, half):
        return Fx.at[chunk, pl.ds(2 * half, 2)]

    def r_part(chunk, half):
        return rq.at[half, chunk]

    def y_piece(chunk, half):
        return Fy.at[chunk, half]

    rs_open(l_part, x, xr, xr_sem, ls, XP, XM)

    def right_partial(index, carry):
        cols = pl.ds(pl.multiple_of(index * RB, RB), RB)
        value = dot3(get(QP, cols), (gwh[:, cols], gwl[:, cols]))
        rpart[index // 2, index % 2] = value.reshape(4, 64, RB)
        return carry

    lax.fori_loop(0, 4, right_partial, 0)
    send(rpart.at[1 - c], rc, rs, rc_sem.at[0], CC)

    rs_mid(l_part, x, xr, xs, xr_sem, ls, XP, XM)
    arrive(rc, rc_sem.at[0])
    rq[...] = rpart[c] + rc[...]
    rs_open(r_part, y, yr, yr_sem, rs, YP, YM)

    first, second = rs_close(l_part, x, xr, xr_sem)
    Q[0:2] = first.reshape(2, 2, 16, LB)
    Q[2:4] = second.reshape(2, 2, 16, LB)
    rs_open(q_part, h, zr, zr_sem, ls, HP, HM)
    rs_mid(r_part, y, yr, ys, yr_sem, rs, YP, YM)
    rs_mid(q_part, h, zr, zs, zr_sem, ls, HP, HM)

    first, second = rs_close(r_part, y, yr, yr_sem)
    ro[0] = first
    ro[1] = second
    send(ro.at[1 - z], rz, rs, rz_sem.at[0], ZZ)

    first, second = rs_close(q_part, h, zr, zr_sem)
    Fx[x, h, 0] = first
    Fx[x, h, 1] = second
    ag_open(z_piece, h, za_sem, ls, HP, HM)

    arrive(rz, rz_sem.at[0])
    Fy[y] = (ro[z] + rz[...]).reshape(2, 32, RB)
    ag_open(y_piece, y, ya_sem, rs, YP, YM)

    ag_mid(z_piece, h, za_sem, ls, HP, HM)
    ag_mid(y_piece, y, ya_sem, rs, YP, YM)
    ag_close(z_piece, h, za_sem)
    ag_open(x_piece, x, xa_sem, ls, XP, XM)
    ag_close(y_piece, y, ya_sem)

    mine = 2 * c + z
    ea, aa, eb = rA.at[4], rA.at[5], rS.at[4]
    rS[5] = Fy[...].reshape(RB, RB)
    diff = adjoint(
        RB, RB, rS.at[5], at(rGP4(rsh, rsl), 4), at(rSP, mine), at(rAP, mine), at(rBP, mine), at(rCT, mine),
        at(rGP4(rah, ral), 4), ea, aa, eb,
    )
    nr_ref[mine] = updated(rp_ref[mine], diff, RB)
    ag_mid(x_piece, x, xa_sem, ls, XP, XM)
    send(nr_ref.at[mine], nr_ref.at[mine], rs, ra_sem.at[mine], ZZ)
    send(nr_ref.at[mine], nr_ref.at[mine], rs, ra_sem.at[mine], CC)
    ag_close(x_piece, x, xa_sem)
    across = 2 * c + 1 - z
    arrive(nr_ref.at[across], ra_sem.at[across])
    send(nr_ref.at[across], nr_ref.at[across], rs, ra_sem.at[across], CC)

    lw[...] = Fx[...].reshape(LB, LB)
    diff = adjoint(
        LB, 256, lw, lGP, lSP, lAP, lBP, lCT, lRP, gw.at[:, 0:LB], gw.at[:, LB : 2 * LB], lA,
    )
    nl_ref[...] = updated(lp_ref[...], diff, LB)

    for zz in (0, 1):
        block = 2 * (1 - c) + zz
        arrive(nr_ref.at[block], ra_sem.at[block])
    for copy in started:
        copy.wait_send()


def rGP4(first, second):
    return (first, second)


def pair_of(shape):
    return [pltpu.VMEM(shape, bf16)] * 2


def comm_call(tok, grad, weight, left_param, right_param):
    vm = pltpu.VMEM
    dma = pltpu.SemaphoreType.DMA
    left = (LB, LB)
    right = (6, RB, RB)
    scratch = [
        vm((16, 512, 256), bf16), vm((16, 256, 1024), bf16), vm((512, 1024), f32),
        *pair_of((512, 1024)), *pair_of((512, 1024)), *pair_of((1024, 512)), vm(left, f32),
        vm(left, f32), vm(left, f32), *pair_of(left), *pair_of(left), *pair_of(left), *pair_of(left), *pair_of(left),
        *pair_of(left), *pair_of(left),
        vm(right, f32), vm(right, f32), *pair_of(right), *pair_of(right), *pair_of(right), *pair_of(right),
        *pair_of(right), *pair_of(right),
        vm((4, 2, 64, LB), f32), vm((6, 64, LB), f32), vm((2, 64, LB), f32), vm((4, 2, 16, LB), f32),
        vm((6, 16, LB), f32), vm((2, 16, LB), f32), vm((4, 4, 2, 16, LB), f32),
        vm((2, 2, 4, 64, RB), f32), vm((2, 4, 64, RB), f32), vm((2, 4, 64, RB), f32), vm((6, 64, RB), f32),
        vm((2, 64, RB), f32), vm((2, 64, RB), f32), vm((64, RB), f32), vm((4, 2, 32, RB), f32),
        dma((16, 2)), dma((40,)), dma((16, 2)), dma((40,)), dma((3,)),
        dma((6,)), dma((6,)), dma((4, 2)), dma((4, 2)), dma((32,)),
        dma((1,)), dma((6,)), dma((1,)), dma((4, 2)), dma((4,)), dma((24,)),
    ]
    whole = pl.BlockSpec(memory_space=pltpu.VMEM)
    hbm = pl.BlockSpec(memory_space=pl.ANY)
    return pl.pallas_call(
        comm_kernel,
        out_shape=(jax.ShapeDtypeStruct(left, f32), jax.ShapeDtypeStruct((4, RB, RB), f32)),
        in_specs=[hbm, hbm, whole, whole, whole],
        out_specs=(whole, whole),
        scratch_shapes=scratch,
        compiler_params=pltpu.CompilerParams(
            collective_id=1, has_side_effects=True, vmem_limit_bytes=60 * 1024 * 1024
        ),
        name="comm",
    )(tok, grad, weight, left_param, right_param)


def final_kernel(
    w_ref, nl_ref, nr_ref, out_ref, nlo_ref, nro_ref,
    lS, lA, lsh, lsl, lah, lal, lbh, lbl, lch, lcl, lrh, lrl,
    rS, rA, rsh, rsl, rah, ral, rbh, rbl, rch, rcl, rrh, rrl,
):
    lSP, lAP, lBP, lCP, lRP = (lsh, lsl), (lah, lal), (lbh, lbl), (lch, lcl), (lrh, lrl)
    rSP, rAP, rBP, rCP, rRP = (rsh, rsl), (rah, ral), (rbh, rbl), (rch, rcl), (rrh, rrl)
    param = nl_ref[...]
    nlo_ref[...] = param
    s = (0.5 / math.sqrt(LB)) * (param - param.T)
    lS[...] = s
    put(lSP, s)
    poly(LB, 256, lS, lSP, lAP, lBP, lCP, lA, lambda rows, value: put(lRP, value, rows))

    def block(index, carry):
        param = nr_ref[index]
        nro_ref[index] = param
        s = (0.5 / math.sqrt(RB)) * (param - param.T)
        rS[...] = s
        put(rSP, s)
        poly(RB, RB, rS, rSP, rAP, rBP, rCP, rA, lambda rows, value: put(rRP, value, rows))
        cols = pl.ds(pl.multiple_of(index * RB, RB), RB)
        turned = dot3(get(lRP), split(w_ref[:, cols]))
        out_ref[:, cols] = dot3(split(turned), get(rRP))
        return carry

    lax.fori_loop(0, 4, block, 0)


def final_call(weight, new_left, new_right):
    vm = pltpu.VMEM
    left, right = (LB, LB), (RB, RB)
    whole = pl.BlockSpec(memory_space=pltpu.VMEM)
    scratch = [
        vm(left, f32), vm(left, f32), *pair_of(left), *pair_of(left), *pair_of(left), *pair_of(left), *pair_of(left),
        vm(right, f32), vm(right, f32), *pair_of(right), *pair_of(right), *pair_of(right), *pair_of(right),
        *pair_of(right),
    ]
    return pl.pallas_call(
        final_kernel,
        out_shape=(
            jax.ShapeDtypeStruct(weight.shape, f32), jax.ShapeDtypeStruct(left, f32),
            jax.ShapeDtypeStruct((4, RB, RB), f32),
        ),
        in_specs=[whole] * 3,
        out_specs=(whole,) * 3,
        scratch_shapes=scratch,
        compiler_params=pltpu.CompilerParams(vmem_limit_bytes=60 * 1024 * 1024),
        name="final",
    )(weight, new_left, new_right)


def body(tokens, grad_out, base_weight, left_param, right_param):
    left = left_param.reshape(LB, LB)
    new_left, new_right = comm_call(tokens.T, grad_out, base_weight, left, right_param)
    rotated, new_left, new_right = final_call(base_weight, new_left, new_right)
    return rotated, new_left.reshape(1, LB, LB), new_right


def solution(mesh):
    return jax.shard_map(
        body,
        mesh=mesh,
        in_specs=(
            P("col", "row"),
            P("row", "col"),
            P("row", "col"),
            P("row", None, None),
            P("col", None, None),
        ),
        out_specs=(P("row", "col"), P("row", None, None), P("col", None, None)),
        check_vma=False,
    )
```

```python
import math

import jax
import jax.numpy as jnp
from jax import lax
from jax.experimental import pallas as pl
from jax.experimental.pallas import tpu as pltpu
from jax.sharding import PartitionSpec as P

step_rate = 0.3
epsilon = 1e-06
f32 = jnp.float32
bf16 = jnp.bfloat16
C2, C3, C4, C5, C6 = 1 / 2, 1 / 6, 1 / 24, 1 / 120, 1 / 720
LB, RB = 512, 256
NN = (((1,), (0,)), ((), ()))
NT = (((1,), (1,)), ((), ()))


def split(value):
    high = value.astype(bf16)
    return high, (value - high.astype(f32)).astype(bf16)


def put(pair, value, where=Ellipsis):
    pair[0][where], pair[1][where] = split(value)


def dot(first, second, dims=NN):
    return lax.dot_general(first, second, dims, preferred_element_type=f32)


def dot3(first, second, dims=NN):
    ah, al = first
    bh, bl = second
    return dot(ah, bh, dims) + (dot(ah, bl, dims) + dot(al, bh, dims))


def get(pair, where=Ellipsis):
    return pair[0][where], pair[1][where]


def rows_loop(total, tile, fn):
    def step(index, carry):
        fn(pl.ds(pl.multiple_of(index * tile, tile), tile))
        return carry

    lax.fori_loop(0, total // tile, step, 0)


def eye(rows, size):
    r = lax.broadcasted_iota(jnp.int32, (rows.size, size), 0) + rows.start
    c = lax.broadcasted_iota(jnp.int32, (rows.size, size), 1)
    return jnp.where(r == c, 1.0, 0.0).astype(f32)


def poly(size, tile, S, SP, AP, BP, CP, Af, finish, CT=None, pause=None):
    def square(rows):
        a = dot3(get(SP, rows), get(SP))
        Af[rows] = a
        put(AP, a, rows)

    rows_loop(size, tile, square)

    def cube(rows):
        b = dot3(get(SP, rows), get(AP))
        put(BP, b, rows)
        s = S[rows]
        a = Af[rows]
        even = C3 * eye(rows, size) + C5 * a
        odd = C4 * s + C6 * b
        put(CP, even + odd, rows)
        if CT is not None:
            put(CT, even - odd, rows)

    rows_loop(size, tile, cube)
    if pause is not None:
        pause()

    def last(rows):
        finish(rows, eye(rows, size) + S[rows] + C2 * Af[rows] + dot3(get(BP, rows), get(CP)))

    rows_loop(size, tile, last)


def adjoint(size, tile, G, GP, SP, AP, BP, CT, EP, Ea, Aa, Eb):
    def first(rows):
        c_bar = -dot3(get(BP, rows), get(GP))
        b_bar = dot3(get(GP, rows), get(CT)) + C6 * c_bar
        put(EP, b_bar, rows)
        g = G[rows]
        Ea[rows] = g + C4 * c_bar
        Aa[rows] = C2 * g + C5 * c_bar

    rows_loop(size, tile, first)
    return adjoint_end(size, tile, GP, SP, AP, EP, Ea, Aa, Eb)


def adjoint_end(size, tile, GP, SP, AP, EP, Ea, Aa, Eb):
    def second(rows):
        Ea[rows] += dot3(get(EP, rows), get(AP))
        Aa[rows] -= dot3(get(SP, rows), get(EP))

    rows_loop(size, tile, second)
    a_bar = Aa[...]
    put(GP, a_bar + a_bar.T)

    def third(rows):
        Eb[rows] = Ea[rows] - dot3(get(GP, rows), get(SP))

    rows_loop(size, tile, third)
    e = Eb[...]
    return e - e.T


def updated(param, diff, size):
    p = (0.5 / math.sqrt(size)) * diff
    mean = jnp.sum(p * p) * (1.0 / (size * size))
    return param - step_rate * p / jnp.sqrt(mean + epsilon)


def comm_kernel(
    tok_hbm, grad_ref, w_hbm, lp_hbm, rp_hbm, wrh_hbm, wrl_hbm, nl_hbm, nr_hbm,
    nl_ref, nr_ref, tok_v, w_ref, lp_ref, rp_ref,
    T, Gr, gw, gwh, gwl, mh, ml, qh, ql, lw,
    lS, lA, lsh, lsl, lah, lal, lbh, lbl, lch, lcl, lth, ltl, lrh, lrl, lgh, lgl,
    rS, rA, rsh, rsl, rah, ral, rbh, rbl, rch, rcl, rth, rtl, rrh, rrl,
    lpart, xr, xs, Q, zr, zs, Fx,
    rpart, rc, rq, yr, ys, ro, rz, Fy,
    t_recv, t_send, g_recv, g_send, loc_sem,
    xr_sem, zr_sem, za_sem, xa_sem, l_send,
    rc_sem, yr_sem, rz_sem, ya_sem, ra_sem, r_send,
):
    row = lax.axis_index("row")
    col = lax.axis_index("col")
    y, z, c = row // 4, (row // 2) % 2, row % 2
    h, x = col // 4, col % 4

    def row_of(yy, zz, cc):
        return (lax.rem(yy + 4, 4) * 2 + zz) * 2 + cc

    def col_of(hh, xx):
        return lax.rem(hh + 4, 4) * 4 + lax.rem(xx + 4, 4)

    YP, YM = {"row": row_of(y + 1, z, c)}, {"row": row_of(y + 3, z, c)}
    ZZ, CC = {"row": row_of(y, 1 - z, c)}, {"row": row_of(y, z, 1 - c)}
    XP, XM = {"col": col_of(h, x + 1)}, {"col": col_of(h, x + 3)}
    HP, HM = {"col": col_of(h + 1, x)}, {"col": col_of(h + 3, x)}
    started = []

    def send(src, dst, sems, recv, dev):
        counter = sems[1]
        copy = pltpu.make_async_remote_copy(
            src_ref=src, dst_ref=dst, send_sem=sems[0].at[counter[0]], recv_sem=recv,
            device_id=dev, device_id_type=pl.DeviceIdType.MESH,
        )
        counter[0] += 1
        copy.start()
        started.append(copy)

    def arrive(dst, recv):
        pltpu.make_async_remote_copy(
            src_ref=dst, dst_ref=dst, send_sem=loc_sem.at[5], recv_sem=recv,
            device_id=CC, device_id_type=pl.DeviceIdType.MESH,
        ).wait_recv()

    ts, gs, ls, rs = (t_send, [0]), (g_send, [0]), (l_send, [0]), (r_send, [0])

    load_tok = pltpu.make_async_copy(tok_hbm, tok_v, loc_sem.at[0])
    load_tok.start()
    barrier = pltpu.get_barrier_semaphore()
    for dev in (YP, YM, ZZ, CC, XP, XM, HP, HM):
        pl.semaphore_signal(barrier, inc=1, device_id=dev, device_id_type=pl.DeviceIdType.MESH)
    load_tok.wait()
    T[col] = tok_v[...].astype(f32).T.astype(bf16)
    pl.semaphore_wait(barrier, 8)

    def t_half(ref, half):
        return ref.at[pl.ds(256 * half, 256)]

    def g_half(ref, half):
        return ref.at[pl.ds(128 * half, 128)]

    def t_go(shard, half, dev):
        piece = t_half(T.at[shard], half)
        send(piece, piece, ts, t_recv.at[shard, half], dev)

    def t_in(shard, half):
        arrive(t_half(T.at[shard], half), t_recv.at[shard, half])

    def g_go(shard, half, dev, own=False):
        src = g_half(grad_ref if own else Gr.at[shard], half)
        send(src, g_half(Gr.at[shard], half), gs, g_recv.at[shard, half], dev)

    def g_in(shard, half):
        arrive(g_half(Gr.at[shard], half), g_recv.at[shard, half])

    for half in (0, 1):
        g_go(row, half, YP, True)
        g_go(row, 1 - half, YM, True)
        t_go(col, half, XP)
        t_go(col, 1 - half, XM)
        t_go(col, half, HP)
        t_go(col, 1 - half, HM)
    for half in (0, 1):
        g_go(row, half, ZZ, True)
    for half in (0, 1):
        g_go(row, half, CC, True)

    loads = [
        pltpu.make_async_copy(src, dst, loc_sem.at[1 + index])
        for index, (src, dst) in enumerate(
            ((rp_hbm, rp_ref), (lp_hbm, lp_ref), (w_hbm, w_ref), (grad_ref, Gr.at[row]))
        )
    ]
    for load in loads:
        load.start()

    def t_pass(shard, half, *devs):
        t_in(shard, half)
        for dev in devs:
            t_go(shard, half, dev)

    def g_pass(shard, half, *devs):
        g_in(shard, half)
        for dev in devs:
            g_go(shard, half, dev)
        g_go(shard, half, CC)

    lSP, lAP, lBP, lCP, lCT = (lsh, lsl), (lah, lal), (lbh, lbl), (lch, lcl), (lth, ltl)
    lRP, lGP = (lrh, lrl), (lgh, lgl)
    MP, QP, GWP = (mh, ml), (qh, ql), (gwh, gwl)

    def at(pair, index):
        return tuple(ref.at[index] for ref in pair)

    rSP, rAP, rBP, rCP, rCT = (rsh, rsl), (rah, ral), (rbh, rbl), (rch, rcl), (rth, rtl)
    rRP = (rrh, rrl)

    def right_one(index, carry, source=rp_ref, other=True):
        param = source[index]
        s = (0.5 / math.sqrt(RB)) * (param - param.T)
        rS[index] = s
        put(at(rSP, index), s)
        poly(
            RB, RB, rS.at[index], at(rSP, index), at(rAP, index), at(rBP, index), at(rCP, index), rA.at[index],
            lambda rows, value: put(at(rRP, index), value, rows), at(rCT, index) if other else None,
        )
        return carry

    def weight_right(rows):
        for index in range(4):
            cols = slice(RB * index, RB * (index + 1))
            m = dot3(split(w_ref[rows, cols]), get(at(rRP, index)))
            put(MP, m.T, (cols, rows))

    def left_weight(index, carry):
        cols = pl.ds(pl.multiple_of(index * 256, 256), 256)
        lw = dot3(get(lRP), split(w_ref[:, cols]))
        put(QP, lw.T, cols)
        return carry

    loads[0].wait()
    lax.fori_loop(0, 2, right_one, 0)
    t_pass(col_of(h, x + 3), 0, XP)
    t_pass(col_of(h, x + 1), 1, XM)
    lax.fori_loop(2, 4, right_one, 0)
    g_pass(row_of(y + 3, z, c), 0, YP)
    g_pass(row_of(y + 1, z, c), 1, YM)
    t_pass(col_of(h + 3, x), 0, XP, XM, HP)
    t_pass(col_of(h + 1, x), 1, XM, XP, HM)
    loads[2].wait()
    rows_loop(LB, 256, weight_right)
    t_pass(col_of(h + 3, x + 3), 0, XP)
    t_pass(col_of(h + 1, x + 1), 1, XM)
    g_pass(row_of(y + 3, z, c), 1)
    g_pass(row_of(y + 1, z, c), 0)
    t_pass(col_of(h + 3, x), 1, XP, XM)
    t_pass(col_of(h + 1, x), 0, XM, XP)
    loads[1].wait()
    param = lp_ref[...]
    s = (0.5 / math.sqrt(LB)) * (param - param.T)
    lS[...] = s
    put(lSP, s)
    other = row_of(y, 1 - z, c)

    def middle():
        t_pass(col_of(h + 3, x + 1), 1, XM)
        t_pass(col_of(h + 1, x + 3), 0, XP)
        g_pass(row_of(y + 2, z, c), 0)
        g_pass(row_of(y + 2, z, c), 1)
        g_pass(other, 0, YP, YM)

    poly(LB, 256, lS, lSP, lAP, lBP, lCP, lA, lambda rows, value: put(lRP, value, rows), lCT, middle)
    lax.fori_loop(0, 4, left_weight, 0)
    t_pass(col_of(h + 2, x), 0, XP, XM)
    t_pass(col_of(h + 2, x), 1, XM, XP)
    g_pass(other, 1, YM, YP)
    loads[3].wait()

    def add_chunks(pieces, start=False, end=False):
        def go(rows):
            total = None if start else gw[rows]
            for k in pieces:
                part = dot(T[k, rows], Gr[k])
                total = part if total is None else total + part
            if end:
                put(GWP, total, rows)
            else:
                gw[rows] = total

        rows_loop(LB, 256, go)

    def both(yy, zz):
        return [row_of(yy, zz, 0), row_of(yy, zz, 1)]

    def partner(yy, zz):
        far = row_of(yy, zz, 1 - c)
        g_in(far, 0)
        g_in(far, 1)

    def t_all(hh):
        for who in range(1, 4):
            for half in (0, 1):
                key = (hh, who, half)
                if key not in seen:
                    t_in(col_of(h + hh, x + who), half)

    seen = {
        (0, 3, 0), (0, 1, 1), (3, 3, 0), (1, 1, 1), (3, 1, 1), (1, 3, 0), (2, 3, 0), (2, 1, 1),
    }
    t_all(0)
    for yy in range(4):
        partner(y + yy, z)
    add_chunks(both(h, z), start=True)
    t_pass(col_of(h + 2, x + 3), 0, XP)
    t_pass(col_of(h + 2, x + 1), 1, XM)
    g_pass(row_of(y + 3, 1 - z, c), 0, YP)
    t_all(3)
    t_all(1)
    add_chunks(both(h + 1, z) + both(h + 3, z))
    g_pass(row_of(y + 1, 1 - z, c), 1, YM)
    g_pass(row_of(y + 1, 1 - z, c), 0)
    g_pass(row_of(y + 3, 1 - z, c), 1)
    t_all(2)
    partner(y, 1 - z)
    add_chunks(both(h + 2, z) + both(y, 1 - z))
    g_pass(row_of(y + 2, 1 - z, c), 0)
    partner(y + 1, 1 - z)
    partner(y + 3, 1 - z)
    add_chunks(both(y + 1, 1 - z) + both(y + 3, 1 - z))
    g_pass(row_of(y + 2, 1 - z, c), 1)
    partner(y + 2, 1 - z)
    add_chunks(both(y + 2, 1 - z), end=True)

    def rs_open(part, me, buf, sem, snd, plus, minus):
        far, nxt, prv = lax.rem(me + 2, 4), lax.rem(me + 1, 4), lax.rem(me + 3, 4)
        send(part(far, 0), buf.at[0], snd, sem.at[0], plus)
        send(part(far, 1), buf.at[1], snd, sem.at[1], minus)
        send(part(nxt, 1), buf.at[2], snd, sem.at[2], plus)
        send(part(prv, 0), buf.at[3], snd, sem.at[3], minus)

    def rs_mid(part, me, buf, stage, sem, snd, plus, minus):
        nxt, prv = lax.rem(me + 1, 4), lax.rem(me + 3, 4)
        arrive(buf.at[0], sem.at[0])
        stage[0] = buf[0] + part(nxt, 0)[...]
        send(stage.at[0], buf.at[4], snd, sem.at[4], plus)
        arrive(buf.at[1], sem.at[1])
        stage[1] = buf[1] + part(prv, 1)[...]
        send(stage.at[1], buf.at[5], snd, sem.at[5], minus)

    def rs_close(part, me, buf, sem):
        for index in range(2, 6):
            arrive(buf.at[index], sem.at[index])
        first = part(me, 0)[...] + (buf[3] + buf[4])
        second = part(me, 1)[...] + (buf[2] + buf[5])
        return first, second

    def ag_open(piece, me, sem, snd, plus, minus):
        for half in (0, 1):
            send(piece(me, half), piece(me, half), snd, sem.at[me, half], plus)
            send(piece(me, 1 - half), piece(me, 1 - half), snd, sem.at[me, 1 - half], minus)

    def ag_mid(piece, me, sem, snd, plus, minus):
        nxt, prv = lax.rem(me + 1, 4), lax.rem(me + 3, 4)
        arrive(piece(prv, 0), sem.at[prv, 0])
        send(piece(prv, 0), piece(prv, 0), snd, sem.at[prv, 0], plus)
        arrive(piece(nxt, 1), sem.at[nxt, 1])
        send(piece(nxt, 1), piece(nxt, 1), snd, sem.at[nxt, 1], minus)

    def ag_close(piece, me, sem):
        far, nxt, prv = lax.rem(me + 2, 4), lax.rem(me + 1, 4), lax.rem(me + 3, 4)
        for who, half in ((prv, 1), (nxt, 0), (far, 0), (far, 1)):
            arrive(piece(who, half), sem.at[who, half])

    class Left:
        def __init__(self, p):
            self.p = p
            self.part = lambda chunk, half: lpart.at[p, chunk, half]
            self.q = lambda chunk, half: Q.at[p, chunk, half]
            self.zp = lambda chunk, half: Fx.at[p, x, chunk, half]
            self.xp = lambda chunk, half: Fx.at[p, chunk, pl.ds(2 * half, 2)]

        def compute(self):
            cols = pl.ds(256 * self.p, 256)

            def go(index, carry):
                rows = pl.ds(pl.multiple_of(index * 256, 256), 256)
                value = dot3(get(GWP, rows), (mh[:, cols], ml[:, cols]))
                lpart[self.p, pl.ds(2 * index, 2)] = value.reshape(2, 2, 64, 256)
                return carry

            lax.fori_loop(0, 2, go, 0)

        def x_open(self):
            rs_open(self.part, x, xr.at[self.p], xr_sem.at[self.p], ls, XP, XM)

        def x_mid(self):
            rs_mid(self.part, x, xr.at[self.p], xs.at[self.p], xr_sem.at[self.p], ls, XP, XM)

        def z_open(self):
            p = self.p
            first, second = rs_close(self.part, x, xr.at[p], xr_sem.at[p])
            Q[p, 0:2] = first.reshape(2, 2, 16, 256)
            Q[p, 2:4] = second.reshape(2, 2, 16, 256)
            rs_open(self.q, h, zr.at[p], zr_sem.at[p], ls, HP, HM)

        def z_mid(self):
            p = self.p
            rs_mid(self.q, h, zr.at[p], zs.at[p], zr_sem.at[p], ls, HP, HM)

        def za_open(self):
            p = self.p
            first, second = rs_close(self.q, h, zr.at[p], zr_sem.at[p])
            Fx[p, x, h, 0] = first
            Fx[p, x, h, 1] = second
            ag_open(self.zp, h, za_sem.at[p], ls, HP, HM)

        def za_mid(self):
            ag_mid(self.zp, h, za_sem.at[self.p], ls, HP, HM)

        def xa_open(self):
            ag_close(self.zp, h, za_sem.at[self.p])
            ag_open(self.xp, x, xa_sem.at[self.p], ls, XP, XM)

        def xa_mid(self):
            ag_mid(self.xp, x, xa_sem.at[self.p], ls, XP, XM)

        def finish(self):
            p = self.p
            ag_close(self.xp, x, xa_sem.at[p])
            value = Fx[p].reshape(LB, 256)
            cols = slice(256 * p, 256 * (p + 1))
            pair = split(value)
            lgh[...], lgl[...] = pair

            def go(index, carry):
                rows = pl.ds(pl.multiple_of(index * 256, 256), 256)
                lA[rows, cols] = -dot3(get(lBP, rows), get(lGP))
                part = dot3(get(lGP, rows), get(lCT, cols))
                lw[rows] = part if p == 0 else lw[rows] + part
                return carry

            lax.fori_loop(0, 2, go, 0)

    def r_part(chunk, half):
        return rq.at[half, chunk]

    def y_piece(chunk, half):
        return Fy.at[chunk, half]

    L0, L1 = Left(0), Left(1)

    def right_partial(index):
        cols = pl.ds(pl.multiple_of(index * RB, RB), RB)
        value = dot3(get(QP, cols), (gwh[:, cols], gwl[:, cols]))
        rpart[index // 2, index % 2] = value.reshape(4, 64, RB)

    L0.compute()
    L0.x_open()
    L1.compute()
    right_partial(2 * (1 - c))
    right_partial(2 * (1 - c) + 1)
    send(rpart.at[1 - c], rc, rs, rc_sem.at[0], CC)
    L0.x_mid()
    L1.x_open()
    right_partial(2 * c)
    right_partial(2 * c + 1)
    arrive(rc, rc_sem.at[0])
    rq[...] = rpart[c] + rc[...]
    rs_open(r_part, y, yr, yr_sem, rs, YP, YM)
    L0.z_open()
    L1.x_mid()
    rs_mid(r_part, y, yr, ys, yr_sem, rs, YP, YM)
    L0.z_mid()
    L1.z_open()
    first, second = rs_close(r_part, y, yr, yr_sem)
    ro[0] = first
    ro[1] = second
    send(ro, rz, rs, rz_sem.at[0], ZZ)
    L0.za_open()
    L1.z_mid()
    arrive(rz, rz_sem.at[0])
    Fy[y] = ro[...] + rz[...]
    ag_open(y_piece, y, ya_sem, rs, YP, YM)
    L0.za_mid()
    L1.za_open()
    ag_mid(y_piece, y, ya_sem, rs, YP, YM)
    L0.xa_open()
    L1.za_mid()
    ag_close(y_piece, y, ya_sem)

    def right_new(zz):
        mine = 2 * c + zz
        rS[5] = Fy[:, zz].reshape(RB, RB)
        put(at(rSP, 4), rS[5])
        diff = adjoint(
            RB, RB, rS.at[5], at(rSP, 4), at(rSP, mine), at(rAP, mine), at(rBP, mine), at(rCT, mine),
            at(rAP, 4), rA.at[4], rA.at[5], rS.at[4],
        )
        nr_ref[mine] = updated(rp_ref[mine], diff, RB)
        send(nr_ref.at[mine], nr_ref.at[mine], rs, ra_sem.at[mine], CC)

    def turn_right(index):
        right_one(index, 0, nr_ref, False)
        cols = pl.ds(pl.multiple_of(index * RB, RB), RB)

        def go(rows):
            gwh[rows, cols], gwl[rows, cols] = split(dot3(split(w_ref[rows, cols]), get(at(rRP, index))))

        rows_loop(LB, 256, go)

    def turn_other(zz):
        index = 2 * (1 - c) + zz
        arrive(nr_ref.at[index], ra_sem.at[index])
        turn_right(index)

    right_new(0)
    L0.xa_mid()
    right_new(1)
    L1.xa_open()
    turn_right(2 * c)
    L0.finish()
    turn_other(0)
    L1.xa_mid()
    turn_right(2 * c + 1)
    turn_other(1)
    outs = [
        pltpu.make_async_copy(src, dst, loc_sem.at[1 + index])
        for index, (src, dst) in enumerate(((nr_ref, nr_hbm), (gwh, wrh_hbm), (gwl, wrl_hbm)))
    ]
    for copy in outs:
        copy.start()
    L1.finish()

    Ea, Aa = gw.at[:, 0:LB], gw.at[:, LB : 2 * LB]

    def join(rows):
        c_bar = lA[rows]
        g = jnp.concatenate([Fx[0, pl.ds(2 * (rows.start // 256), 2)].reshape(256, 256),
                             Fx[1, pl.ds(2 * (rows.start // 256), 2)].reshape(256, 256)], axis=1)
        put(lRP, lw[rows] + C6 * c_bar, rows)
        Ea[rows] = g + C4 * c_bar
        Aa[rows] = C2 * g + C5 * c_bar

    join(pl.ds(0, 256))
    join(pl.ds(256, 256))
    diff = adjoint_end(LB, 256, lCP, lSP, lAP, lRP, Ea, Aa, lA)
    nl_ref[...] = updated(lp_ref[...], diff, LB)
    put_left = pltpu.make_async_copy(nl_ref, nl_hbm, loc_sem.at[0])
    put_left.start()

    for copy in started:
        copy.wait_send()
    for copy in [put_left] + outs:
        copy.wait()


def pair_of(shape):
    return [pltpu.VMEM(shape, bf16)] * 2


def comm_call(tok, grad, weight, left_param, right_param):
    vm = pltpu.VMEM
    dma = pltpu.SemaphoreType.DMA
    left = (LB, LB)
    right = (6, RB, RB)
    scratch = [
        vm(left, f32), vm((4, RB, RB), f32), vm((256, 512), bf16), vm((512, 1024), f32), vm(left, f32),
        vm((4, RB, RB), f32),
        vm((16, 512, 256), bf16), vm((16, 256, 1024), bf16), vm((512, 1024), f32),
        *pair_of((512, 1024)), *pair_of((1024, 512)), *pair_of((1024, 512)), vm(left, f32),
        vm(left, f32), vm(left, f32), *pair_of(left), *pair_of(left), *pair_of(left), *pair_of(left), *pair_of(left),
        *pair_of(left), *pair_of((512, 256)),
        vm(right, f32), vm(right, f32), *pair_of(right), *pair_of(right), *pair_of(right), *pair_of(right),
        *pair_of(right), *pair_of(right),
        vm((2, 4, 2, 64, 256), f32), vm((2, 6, 64, 256), f32), vm((2, 2, 64, 256), f32), vm((2, 4, 2, 16, 256), f32),
        vm((2, 6, 16, 256), f32), vm((2, 2, 16, 256), f32), vm((2, 4, 4, 2, 16, 256), f32),
        vm((2, 2, 4, 64, RB), f32), vm((2, 4, 64, RB), f32), vm((2, 4, 64, RB), f32), vm((6, 64, RB), f32),
        vm((2, 64, RB), f32), vm((2, 64, RB), f32), vm((2, 64, RB), f32), vm((4, 2, 64, RB), f32),
        dma((16, 2)), dma((30,)), dma((16, 2)), dma((30,)), dma((6,)),
        dma((2, 6)), dma((2, 6)), dma((2, 4, 2)), dma((2, 4, 2)), dma((48,)),
        dma((1,)), dma((6,)), dma((1,)), dma((4, 2)), dma((4,)), dma((24,)),
    ]
    hbm = pl.BlockSpec(memory_space=pl.ANY)
    return pl.pallas_call(
        comm_kernel,
        out_shape=(
            jax.ShapeDtypeStruct(weight.shape, bf16), jax.ShapeDtypeStruct(weight.shape, bf16),
            jax.ShapeDtypeStruct(left, f32),
            jax.ShapeDtypeStruct((4, RB, RB), f32),
        ),
        in_specs=[hbm] * 5,
        out_specs=(hbm,) * 4,
        scratch_shapes=scratch,
        compiler_params=pltpu.CompilerParams(
            collective_id=1, has_side_effects=True, vmem_limit_bytes=60 * 1024 * 1024
        ),
        name="comm",
    )(tok, grad, weight, left_param, right_param)


def final_kernel(
    wrh, wrl, nl, nr, out, nlo, nro, wh, wl, acc, nl_v, nr_v, S, A, sh, sl, ah, al, bh, bl, ch, cl, rh, rl, sem
):
    def copy(src, dst, index):
        made = pltpu.make_async_copy(src, dst, sem.at[index])
        made.start()
        return made

    left_in = copy(nl, nl_v, 0)
    right_in = copy(nr, nr_v, 1)
    weight_in = [copy(wrh, wh, 2), copy(wrl, wl, 3)]
    left_in.wait()
    outs = [copy(nl_v, nlo, 4)]
    param = nl_v[...]
    s = (0.5 / math.sqrt(LB)) * (param - param.T)
    S[...] = s
    put((sh, sl), s)
    right_in.wait()
    outs.append(copy(nr_v, nro, 5))
    poly(
        LB, 256, S, (sh, sl), (ah, al), (bh, bl), (ch, cl), A, lambda rows, value: put((rh, rl), value, rows)
    )
    for made in weight_in:
        made.wait()
    for index in range(4):
        cols = pl.ds(256 * index, 256)
        acc[:, cols] = dot3((rh[...], rl[...]), (wh[:, cols], wl[:, cols]))
        outs.append(copy(acc.at[:, cols], out.at[:, cols], 6 + index))
    for made in outs:
        made.wait()


def final_call(wrh, wrl, new_left, new_right):
    vm = pltpu.VMEM
    hbm = pl.BlockSpec(memory_space=pl.ANY)
    left = (LB, LB)
    return pl.pallas_call(
        final_kernel,
        out_shape=(
            jax.ShapeDtypeStruct(wrh.shape, f32), jax.ShapeDtypeStruct(left, f32),
            jax.ShapeDtypeStruct((4, RB, RB), f32),
        ),
        in_specs=[hbm] * 4,
        out_specs=(hbm,) * 3,
        scratch_shapes=[
            *pair_of(wrh.shape), vm(wrh.shape, f32), vm(left, f32), vm((4, RB, RB), f32), vm(left, f32), vm(left, f32),
            *pair_of(left), *pair_of(left), *pair_of(left), *pair_of(left), *pair_of(left),
            pltpu.SemaphoreType.DMA((10,)),
        ],
        compiler_params=pltpu.CompilerParams(vmem_limit_bytes=60 * 1024 * 1024),
        name="final",
    )(wrh, wrl, new_left, new_right)


def body(tokens, grad_out, base_weight, left_param, right_param):
    left = left_param.reshape(LB, LB)
    given = comm_call(tokens, grad_out, base_weight, left, right_param)
    rotated, new_left, new_right = final_call(*given)
    return rotated, new_left.reshape(1, LB, LB), new_right


def solution(mesh):
    return jax.shard_map(
        body,
        mesh=mesh,
        in_specs=(
            P("col", "row"),
            P("row", "col"),
            P("row", "col"),
            P("row", None, None),
            P("col", None, None),
        ),
        out_specs=(P("row", "col"), P("row", None, None), P("col", None, None)),
        check_vma=False,
    )
```

```python
import math

import jax
import jax.numpy as jnp
from jax import lax
from jax.experimental import pallas as pl
from jax.experimental.pallas import tpu as pltpu
from jax.sharding import PartitionSpec as P

step_rate = 0.3
epsilon = 1e-06
f32 = jnp.float32
bf16 = jnp.bfloat16
C2, C3, C4, C5, C6 = 1 / 2, 1 / 6, 1 / 24, 1 / 120, 1 / 720
LB, RB = 512, 256
NN = (((1,), (0,)), ((), ()))
NT = (((1,), (1,)), ((), ()))


def split(value):
    high = value.astype(bf16)
    return high, (value - high.astype(f32)).astype(bf16)


def put(pair, value, where=Ellipsis):
    pair[0][where], pair[1][where] = split(value)


def dot(first, second, dims=NN):
    return lax.dot_general(first, second, dims, preferred_element_type=f32)


def dot3(first, second, dims=NN):
    ah, al = first
    bh, bl = second
    return dot(ah, bh, dims) + (dot(ah, bl, dims) + dot(al, bh, dims))


def get(pair, where=Ellipsis):
    return pair[0][where], pair[1][where]


def rows_loop(total, tile, fn):
    def step(index, carry):
        fn(pl.ds(pl.multiple_of(index * tile, tile), tile))
        return carry

    lax.fori_loop(0, total // tile, step, 0)


def eye(rows, size):
    r = lax.broadcasted_iota(jnp.int32, (rows.size, size), 0) + rows.start
    c = lax.broadcasted_iota(jnp.int32, (rows.size, size), 1)
    return jnp.where(r == c, 1.0, 0.0).astype(f32)


def poly(size, tile, S, SP, AP, BP, CP, Af, finish, CT=None, pause=None, early=None):
    def square(rows):
        a = dot3(get(SP, rows), get(SP))
        Af[rows] = a
        put(AP, a, rows)

    rows_loop(size, tile, square)
    if early is not None:
        early()

    def cube(rows):
        b = dot3(get(SP, rows), get(AP))
        put(BP, b, rows)
        s = S[rows]
        a = Af[rows]
        even = C3 * eye(rows, size) + C5 * a
        odd = C4 * s + C6 * b
        put(CP, even + odd, rows)
        if CT is not None:
            put(CT, even - odd, rows)

    rows_loop(size, tile, cube)
    if pause is not None:
        pause()

    def last(rows):
        finish(rows, eye(rows, size) + S[rows] + C2 * Af[rows] + dot3(get(BP, rows), get(CP)))

    rows_loop(size, tile, last)


def adjoint(size, tile, G, GP, SP, AP, BP, CT, EP, Ea, Aa, Eb):
    def first(rows):
        c_bar = -dot3(get(BP, rows), get(GP))
        b_bar = dot3(get(GP, rows), get(CT)) + C6 * c_bar
        put(EP, b_bar, rows)
        g = G[rows]
        Ea[rows] = g + C4 * c_bar
        Aa[rows] = C2 * g + C5 * c_bar

    rows_loop(size, tile, first)
    return adjoint_end(size, tile, GP, SP, AP, EP, Ea, Aa, Eb)


def adjoint_end(size, tile, GP, SP, AP, EP, Ea, Aa, Eb):
    def second(rows):
        Ea[rows] += dot3(get(EP, rows), get(AP))
        Aa[rows] -= dot3(get(SP, rows), get(EP))

    rows_loop(size, tile, second)
    a_bar = Aa[...]
    put(GP, a_bar + a_bar.T)

    def third(rows):
        Eb[rows] = Ea[rows] - dot3(get(GP, rows), get(SP))

    rows_loop(size, tile, third)
    e = Eb[...]
    return e - e.T


def updated(param, diff, size):
    p = (0.5 / math.sqrt(size)) * diff
    mean = jnp.sum(p * p) * (1.0 / (size * size))
    return param - step_rate * p / jnp.sqrt(mean + epsilon)


def comm_kernel(
    tok_hbm, grad_ref, w_hbm, lp_hbm, rp_hbm, gwh, gwl, nl_ref, nr_hbm,
    nr_ref, tok_v, w_ref, lp_ref, rp_ref,
    T, Gr, gw, mh, ml, qh, ql,
    lS, lA, lsh, lsl, lah, lal, lbh, lbl, lch, lcl, lth, ltl, lrh, lrl, lgh, lgl,
    rS, rA, rsh, rsl, rah, ral, rbh, rbl, rch, rcl, rth, rtl, rrh, rrl,
    lpart, xr, xs, Q, zr, zs, Fx,
    rpart, rc, rq, yr, ys, ro, rz, Fy,
    t_recv, t_send, g_recv, g_send, loc_sem,
    xr_sem, zr_sem, za_sem, xa_sem, l_send,
    rc_sem, yr_sem, rz_sem, ya_sem, ra_sem, rb_sem, r_send,
):
    row = lax.axis_index("row")
    col = lax.axis_index("col")
    y, z, c = row // 4, (row // 2) % 2, row % 2
    h, x = col // 4, col % 4

    def row_of(yy, zz, cc):
        return (lax.rem(yy + 4, 4) * 2 + zz) * 2 + cc

    def col_of(hh, xx):
        return lax.rem(hh + 4, 4) * 4 + lax.rem(xx + 4, 4)

    YP, YM = {"row": row_of(y + 1, z, c)}, {"row": row_of(y + 3, z, c)}
    ZZ, CC = {"row": row_of(y, 1 - z, c)}, {"row": row_of(y, z, 1 - c)}
    XP, XM = {"col": col_of(h, x + 1)}, {"col": col_of(h, x + 3)}
    HP, HM = {"col": col_of(h + 1, x)}, {"col": col_of(h + 3, x)}
    started = []

    def send(src, dst, sems, recv, dev):
        counter = sems[1]
        copy = pltpu.make_async_remote_copy(
            src_ref=src, dst_ref=dst, send_sem=sems[0].at[counter[0]], recv_sem=recv,
            device_id=dev, device_id_type=pl.DeviceIdType.MESH,
        )
        counter[0] += 1
        copy.start()
        started.append(copy)

    def arrive(dst, recv):
        pltpu.make_async_remote_copy(
            src_ref=dst, dst_ref=dst, send_sem=loc_sem.at[5], recv_sem=recv,
            device_id=CC, device_id_type=pl.DeviceIdType.MESH,
        ).wait_recv()

    ts, gs, ls, rs = (t_send, [0]), (g_send, [0]), (l_send, [0]), (r_send, [0])

    load_tok = pltpu.make_async_copy(tok_hbm, tok_v, loc_sem.at[0])
    load_tok.start()
    barrier = pltpu.get_barrier_semaphore()
    for dev in (YP, YM, ZZ, CC, XP, XM, HP, HM):
        pl.semaphore_signal(barrier, inc=1, device_id=dev, device_id_type=pl.DeviceIdType.MESH)
    load_tok.wait()
    T[col] = tok_v[...].astype(f32).T.astype(bf16)
    pl.semaphore_wait(barrier, 8)

    def t_half(ref, half):
        return ref.at[pl.ds(256 * half, 256)]

    def g_half(ref, half):
        return ref.at[pl.ds(64 * half, 64)]

    def t_go(shard, half, dev):
        piece = t_half(T.at[shard], half)
        send(piece, piece, ts, t_recv.at[shard, half], dev)

    def t_in(shard, half):
        arrive(t_half(T.at[shard], half), t_recv.at[shard, half])

    def g_go(shard, half, dev, own=False):
        src = g_half(grad_ref if own else Gr.at[shard], half)
        send(src, g_half(Gr.at[shard], half), gs, g_recv.at[shard, half], dev)

    def g_in(shard, half):
        arrive(g_half(Gr.at[shard], half), g_recv.at[shard, half])

    for half in (0, 1):
        t_go(col, half, XP)
        t_go(col, 1 - half, XM)
        t_go(col, half, HP)
        t_go(col, 1 - half, HM)
    for q in range(4):
        g_go(row, q, YP, True)
        g_go(row, (q + 2) % 4, YM, True)
    for q in (0, 2, 1):
        g_go(row, q, ZZ, True)
    for q in range(4):
        g_go(row, q, CC, True)

    loads = [
        pltpu.make_async_copy(src, dst, loc_sem.at[1 + index])
        for index, (src, dst) in enumerate(
            ((rp_hbm, rp_ref), (lp_hbm, lp_ref), (w_hbm, w_ref), (grad_ref, Gr.at[row]))
        )
    ]
    for load in loads:
        load.start()

    def t_pass(shard, half, *devs):
        t_in(shard, half)
        for dev in devs:
            t_go(shard, half, dev)

    def g_pass(shard, half, *devs):
        g_in(shard, half)
        for dev in devs:
            g_go(shard, half, dev)
        g_go(shard, half, CC)

    lSP, lAP, lBP, lCP, lCT = (lsh, lsl), (lah, lal), (lbh, lbl), (lch, lcl), (lth, ltl)
    lRP, lGP = (lrh, lrl), (lgh, lgl)
    MP, QP, GWP = (mh, ml), (qh, ql), (gwh, gwl)

    def at(pair, index):
        return tuple(ref.at[index] for ref in pair)

    rSP, rAP, rBP, rCP, rCT = (rsh, rsl), (rah, ral), (rbh, rbl), (rch, rcl), (rth, rtl)
    rRP = (rrh, rrl)

    def right_one(index, carry, source=rp_ref, other=True):
        param = source[index]
        s = (0.5 / math.sqrt(RB)) * (param - param.T)
        rS[index] = s
        put(at(rSP, index), s)
        poly(
            RB, RB, rS.at[index], at(rSP, index), at(rAP, index), at(rBP, index), at(rCP, 0), rA.at[index],
            lambda rows, value: put(at(rRP, index), value, rows), at(rCT, index) if other else None,
        )
        return carry

    def weight_right(rows):
        for index in range(4):
            cols = slice(RB * index, RB * (index + 1))
            m = dot3(split(w_ref[rows, cols]), get(at(rRP, index)))
            put(MP, m.T, (cols, rows))

    def left_weight(index, carry):
        cols = pl.ds(pl.multiple_of(index * 256, 256), 256)
        lw = dot3(get(lRP), split(w_ref[:, cols]))
        put(QP, lw.T, cols)
        return carry

    up, down, far = y + 1, y + 3, y + 2
    other = row_of(y, 1 - z, c)

    def g_up(q, zz, *devs):
        g_pass(row_of(up, zz, c), q, *devs)

    def g_down(q, zz, *devs):
        g_pass(row_of(down, zz, c), q, *devs)

    def g_far(q, zz):
        g_pass(row_of(far, zz, c), q)

    loads[0].wait()
    lax.fori_loop(0, 4, right_one, 0)
    t_pass(col_of(h, x + 3), 0, XP)
    t_pass(col_of(h, x + 1), 1, XM)
    g_down(0, z, YP)
    g_up(2, z, YM)
    loads[2].wait()
    weight_right(pl.ds(0, 256))
    g_down(1, z, YP)
    g_up(3, z, YM)
    t_pass(col_of(h + 3, x), 0, XP, XM, HP)
    t_pass(col_of(h + 1, x), 1, XM, XP, HM)
    g_go(row, 3, ZZ, True)
    weight_right(pl.ds(256, 256))
    loads[1].wait()
    param = lp_ref[...]
    s = (0.5 / math.sqrt(LB)) * (param - param.T)
    lS[...] = s
    put(lSP, s)
    g_down(2, z)
    g_up(0, z)

    def early():
        g_down(3, z)
        g_up(1, z)
        t_pass(col_of(h + 3, x + 3), 0, XP)
        t_pass(col_of(h + 1, x + 1), 1, XM)
        t_pass(col_of(h + 3, x), 1, XM, XP)
        t_pass(col_of(h + 1, x), 0, XP, XM)

    def middle():
        g_far(0, z)
        g_far(2, z)
        g_pass(other, 0, YP, YM)

    poly(LB, 256, lS, lSP, lAP, lBP, lCP, lA, lambda rows, value: put(lRP, value, rows), lCT, middle, early)
    g_far(1, z)
    g_far(3, z)
    g_pass(other, 2, YM, YP)
    lax.fori_loop(0, 4, left_weight, 0)
    g_down(0, 1 - z, YP)
    g_pass(other, 1, YP, YM)
    t_pass(col_of(h + 3, x + 1), 1, XM)
    t_pass(col_of(h + 1, x + 3), 0, XP)
    g_up(2, 1 - z, YM)
    loads[3].wait()

    def add_chunks(pieces, start=False, end=False):
        def go(rows):
            total = None if start else gw[rows]
            for k in pieces:
                part = dot(T[k, rows], Gr[k])
                total = part if total is None else total + part
            if end:
                put(GWP, total, rows)
            else:
                gw[rows] = total

        rows_loop(LB, 256, go)

    def both(yy, zz):
        return [row_of(yy, zz, 0), row_of(yy, zz, 1)]

    def partner(yy, zz):
        far = row_of(yy, zz, 1 - c)
        for q in range(4):
            g_in(far, q)

    def t_all(hh):
        for who in range(1, 4):
            for half in (0, 1):
                key = (hh, who, half)
                if key not in seen:
                    t_in(col_of(h + hh, x + who), half)

    seen = {
        (0, 3, 0), (0, 1, 1), (3, 3, 0), (1, 1, 1), (3, 1, 1), (1, 3, 0), (2, 3, 0), (2, 1, 1),
    }
    t_all(0)
    for yy in range(4):
        partner(y + yy, z)
    add_chunks(both(h, z), start=True)
    t_pass(col_of(h + 2, x), 0, XP, XM)
    t_pass(col_of(h + 2, x), 1, XM, XP)
    g_down(1, 1 - z, YP)
    t_all(3)
    t_all(1)
    add_chunks(both(h + 1, z))
    g_pass(other, 3, YM, YP)
    g_up(0, 1 - z)
    g_down(2, 1 - z)
    add_chunks(both(h + 3, z))
    t_pass(col_of(h + 2, x + 3), 0, XP)
    t_pass(col_of(h + 2, x + 1), 1, XM)
    g_up(1, 1 - z)
    g_far(0, 1 - z)
    g_far(2, 1 - z)
    g_up(3, 1 - z, YM)
    g_down(3, 1 - z)
    g_far(1, 1 - z)
    t_all(2)
    partner(y, 1 - z)
    add_chunks(both(h + 2, z) + both(y, 1 - z))
    partner(y + 1, 1 - z)
    partner(y + 3, 1 - z)
    add_chunks(both(y + 1, 1 - z) + both(y + 3, 1 - z))
    g_far(3, 1 - z)
    partner(y + 2, 1 - z)
    add_chunks(both(y + 2, 1 - z), end=True)

    def rs_open(part, me, buf, sem, snd, plus, minus):
        far = lax.rem(me + 2, 4)
        send(part(far, 0), buf.at[0], snd, sem.at[0], plus)
        send(part(far, 1), buf.at[1], snd, sem.at[1], minus)

    def rs_single(part, me, buf, sem, snd, plus, minus):
        nxt, prv = lax.rem(me + 1, 4), lax.rem(me + 3, 4)
        send(part(nxt, 1), buf.at[2], snd, sem.at[2], plus)
        send(part(prv, 0), buf.at[3], snd, sem.at[3], minus)

    def rs_mid(part, me, buf, stage, sem, snd, plus, minus):
        nxt, prv = lax.rem(me + 1, 4), lax.rem(me + 3, 4)
        arrive(buf.at[0], sem.at[0])
        stage[0] = buf[0] + part(nxt, 0)[...]
        send(stage.at[0], buf.at[4], snd, sem.at[4], plus)
        arrive(buf.at[1], sem.at[1])
        stage[1] = buf[1] + part(prv, 1)[...]
        send(stage.at[1], buf.at[5], snd, sem.at[5], minus)

    def rs_close(part, me, buf, sem):
        for index in range(2, 6):
            arrive(buf.at[index], sem.at[index])
        first = part(me, 0)[...] + (buf[3] + buf[4])
        second = part(me, 1)[...] + (buf[2] + buf[5])
        return first, second

    def ag_open(piece, me, sem, snd, plus, minus):
        for half in (0, 1):
            send(piece(me, half), piece(me, half), snd, sem.at[me, half], plus)
            send(piece(me, 1 - half), piece(me, 1 - half), snd, sem.at[me, 1 - half], minus)

    def ag_mid(piece, me, sem, snd, plus, minus):
        nxt, prv = lax.rem(me + 1, 4), lax.rem(me + 3, 4)
        arrive(piece(prv, 0), sem.at[prv, 0])
        send(piece(prv, 0), piece(prv, 0), snd, sem.at[prv, 0], plus)
        arrive(piece(nxt, 1), sem.at[nxt, 1])
        send(piece(nxt, 1), piece(nxt, 1), snd, sem.at[nxt, 1], minus)

    def ag_close(piece, me, sem):
        far, nxt, prv = lax.rem(me + 2, 4), lax.rem(me + 1, 4), lax.rem(me + 3, 4)
        for who, half in ((prv, 1), (nxt, 0), (far, 0), (far, 1)):
            arrive(piece(who, half), sem.at[who, half])

    class Left:
        def __init__(self, p):
            self.p = p
            self.part = lambda chunk, half: lpart.at[p, chunk, half]
            self.q = lambda chunk, half: Q.at[p, chunk, half]
            self.zp = lambda chunk, half: Fx.at[p, x, chunk, half]
            self.xp = lambda chunk, half: Fx.at[p, chunk, pl.ds(2 * half, 2)]

        def compute(self):
            cols = pl.ds(256 * self.p, 256)

            def go(index, carry):
                rows = pl.ds(pl.multiple_of(index * 256, 256), 256)
                value = dot3(get(GWP, rows), (mh[:, cols], ml[:, cols]))
                lpart[self.p, pl.ds(2 * index, 2)] = value.reshape(2, 2, 64, 256)
                return carry

            lax.fori_loop(0, 2, go, 0)

        def x_open(self):
            rs_open(self.part, x, xr.at[self.p], xr_sem.at[self.p], ls, XP, XM)

        def x_single(self):
            rs_single(self.part, x, xr.at[self.p], xr_sem.at[self.p], ls, XP, XM)

        def x_mid(self):
            rs_mid(self.part, x, xr.at[self.p], xs.at[self.p], xr_sem.at[self.p], ls, XP, XM)

        def z_open(self):
            p = self.p
            first, second = rs_close(self.part, x, xr.at[p], xr_sem.at[p])
            Q[p, 0:2] = first.reshape(2, 2, 16, 256)
            Q[p, 2:4] = second.reshape(2, 2, 16, 256)
            rs_open(self.q, h, zr.at[p], zr_sem.at[p], ls, HP, HM)
            rs_single(self.q, h, zr.at[p], zr_sem.at[p], ls, HP, HM)

        def z_mid(self):
            p = self.p
            rs_mid(self.q, h, zr.at[p], zs.at[p], zr_sem.at[p], ls, HP, HM)

        def za_open(self):
            p = self.p
            first, second = rs_close(self.q, h, zr.at[p], zr_sem.at[p])
            Fx[p, x, h, 0] = first
            Fx[p, x, h, 1] = second
            ag_open(self.zp, h, za_sem.at[p], ls, HP, HM)

        def za_mid(self):
            ag_mid(self.zp, h, za_sem.at[self.p], ls, HP, HM)

        def xa_open(self):
            ag_close(self.zp, h, za_sem.at[self.p])
            ag_open(self.xp, x, xa_sem.at[self.p], ls, XP, XM)

        def xa_mid(self):
            ag_mid(self.xp, x, xa_sem.at[self.p], ls, XP, XM)

        def finish(self):
            p = self.p
            ag_close(self.xp, x, xa_sem.at[p])
            value = Fx[p].reshape(LB, 256)
            cols = slice(256 * p, 256 * (p + 1))
            pair = split(value)
            lgh[...], lgl[...] = pair

            def go(index, carry):
                rows = pl.ds(pl.multiple_of(index * 256, 256), 256)
                lA[rows, cols] = -dot3(get(lBP, rows), get(lGP))
                part = dot3(get(lGP, rows), get(lCT, cols))
                lw[rows] = part if p == 0 else lw[rows] + part
                return carry

            lax.fori_loop(0, 2, go, 0)

    def r_part(chunk, half):
        return rq.at[half, chunk]

    def y_piece(chunk, half):
        return Fy.at[chunk, half]

    lw = gw.at[:, LB : 2 * LB]
    L0, L1 = Left(0), Left(1)

    def right_partial(index):
        cols = pl.ds(pl.multiple_of(index * RB, RB), RB)
        value = dot3(get(QP, cols), (gwh[:, cols], gwl[:, cols]))
        rpart[index // 2, index % 2] = value.reshape(4, 64, RB)

    L0.compute()
    L0.x_open()
    L1.compute()
    L1.x_open()
    L0.x_single()
    right_partial(2 * (1 - c))
    right_partial(2 * (1 - c) + 1)
    send(rpart.at[1 - c], rc, rs, rc_sem.at[0], CC)
    right_partial(2 * c)
    right_partial(2 * c + 1)
    L0.x_mid()
    L1.x_single()
    arrive(rc, rc_sem.at[0])
    rq[...] = rpart[c] + rc[...]
    rs_open(r_part, y, yr, yr_sem, rs, YP, YM)
    rs_single(r_part, y, yr, yr_sem, rs, YP, YM)
    L1.x_mid()
    L0.z_open()
    rs_mid(r_part, y, yr, ys, yr_sem, rs, YP, YM)
    L1.z_open()
    L0.z_mid()
    first, second = rs_close(r_part, y, yr, yr_sem)
    ro[0] = first
    ro[1] = second
    send(ro, rz, rs, rz_sem.at[0], ZZ)
    L1.z_mid()
    L0.za_open()
    L1.za_open()
    arrive(rz, rz_sem.at[0])
    Fy[y] = ro[...] + rz[...]
    ag_open(y_piece, y, ya_sem, rs, YP, YM)
    L0.za_mid()
    L1.za_mid()
    ag_mid(y_piece, y, ya_sem, rs, YP, YM)
    L0.xa_open()
    L1.xa_open()
    ag_close(y_piece, y, ya_sem)

    def right_new(zz):
        mine = 2 * c + zz
        rS[5] = Fy[:, zz].reshape(RB, RB)
        put(at(rSP, 4), rS[5])
        diff = adjoint(
            RB, RB, rS.at[5], at(rSP, 4), at(rSP, mine), at(rAP, mine), at(rBP, mine), at(rCT, mine),
            at(rAP, 4), rA.at[4], rA.at[5], rS.at[4],
        )
        nr_ref[mine] = updated(rp_ref[mine], diff, RB)
        send(nr_ref.at[mine], nr_ref.at[mine], rs, ra_sem.at[mine], CC)

    def new_rotation(zz):
        mine = 2 * c + zz
        right_one(mine, 0, nr_ref, False)
        send(rrh.at[mine], rrh.at[mine], rs, rb_sem.at[mine, 0], CC)
        send(rrl.at[mine], rrl.at[mine], rs, rb_sem.at[mine, 1], CC)

    def turn_right(index):
        cols = pl.ds(pl.multiple_of(index * RB, RB), RB)

        def go(rows):
            gwh[rows, cols], gwl[rows, cols] = split(dot3(split(w_ref[rows, cols]), get(at(rRP, index))))

        rows_loop(LB, 256, go)

    def turn_other(zz):
        index = 2 * (1 - c) + zz
        arrive(rrh.at[index], rb_sem.at[index, 0])
        arrive(rrl.at[index], rb_sem.at[index, 1])
        turn_right(index)

    right_new(0)
    L0.xa_mid()
    right_new(1)
    new_rotation(0)
    new_rotation(1)
    L1.xa_mid()
    turn_right(2 * c)
    turn_right(2 * c + 1)
    L0.finish()
    turn_other(0)
    turn_other(1)
    for zz in (0, 1):
        arrive(nr_ref.at[2 * (1 - c) + zz], ra_sem.at[2 * (1 - c) + zz])
    put_right = pltpu.make_async_copy(nr_ref, nr_hbm, loc_sem.at[0])
    put_right.start()
    L1.finish()

    Ea, Aa = gw.at[:, 0:LB], gw.at[:, LB : 2 * LB]

    def join(rows):
        c_bar = lA[rows]
        g = jnp.concatenate([Fx[0, pl.ds(2 * (rows.start // 256), 2)].reshape(256, 256),
                             Fx[1, pl.ds(2 * (rows.start // 256), 2)].reshape(256, 256)], axis=1)
        put(lRP, lw[rows] + C6 * c_bar, rows)
        Ea[rows] = g + C4 * c_bar
        Aa[rows] = C2 * g + C5 * c_bar

    join(pl.ds(0, 256))
    join(pl.ds(256, 256))
    diff = adjoint_end(LB, 256, lCP, lSP, lAP, lRP, Ea, Aa, lA)
    nl_ref[...] = updated(lp_ref[...], diff, LB)

    for copy in started:
        copy.wait_send()
    put_right.wait()


def pair_of(shape):
    return [pltpu.VMEM(shape, bf16)] * 2


def comm_call(tok, grad, weight, left_param, right_param):
    vm = pltpu.VMEM
    dma = pltpu.SemaphoreType.DMA
    left = (LB, LB)
    right = (6, RB, RB)
    scratch = [
        vm((4, RB, RB), f32), vm((256, 512), bf16), vm((512, 1024), f32), vm(left, f32),
        vm((4, RB, RB), f32),
        vm((16, 512, 256), bf16), vm((16, 256, 1024), bf16), vm((512, 1024), f32),
        *pair_of((1024, 512)), *pair_of((1024, 512)),
        vm(left, f32), vm(left, f32), *pair_of(left), *pair_of(left), *pair_of(left), *pair_of(left), *pair_of(left),
        *pair_of(left), *pair_of((512, 256)),
        vm(right, f32), vm(right, f32), *pair_of((5, RB, RB)), *pair_of((5, RB, RB)), *pair_of((4, RB, RB)),
        *pair_of((1, RB, RB)), *pair_of((4, RB, RB)), *pair_of((4, RB, RB)),
        vm((2, 4, 2, 64, 256), f32), vm((2, 6, 64, 256), f32), vm((2, 2, 64, 256), f32), vm((2, 4, 2, 16, 256), f32),
        vm((2, 6, 16, 256), f32), vm((2, 2, 16, 256), f32), vm((2, 4, 4, 2, 16, 256), f32),
        vm((2, 2, 4, 64, RB), f32), vm((2, 4, 64, RB), f32), vm((2, 4, 64, RB), f32), vm((6, 64, RB), f32),
        vm((2, 64, RB), f32), vm((2, 64, RB), f32), vm((2, 64, RB), f32), vm((4, 2, 64, RB), f32),
        dma((16, 2)), dma((30,)), dma((16, 4)), dma((60,)), dma((6,)),
        dma((2, 6)), dma((2, 6)), dma((2, 4, 2)), dma((2, 4, 2)), dma((48,)),
        dma((1,)), dma((6,)), dma((1,)), dma((4, 2)), dma((4,)), dma((4, 2)), dma((24,)),
    ]
    hbm = pl.BlockSpec(memory_space=pltpu.HBM)
    vmem = pl.BlockSpec(memory_space=pltpu.VMEM)
    return pl.pallas_call(
        comm_kernel,
        out_shape=(
            jax.ShapeDtypeStruct(weight.shape, bf16), jax.ShapeDtypeStruct(weight.shape, bf16),
            jax.ShapeDtypeStruct(left, f32),
            jax.ShapeDtypeStruct((4, RB, RB), f32),
        ),
        in_specs=[hbm] * 5,
        out_specs=(vmem, vmem, vmem, hbm),
        scratch_shapes=scratch,
        compiler_params=pltpu.CompilerParams(
            collective_id=1, has_side_effects=True, vmem_limit_bytes=50 * 1024 * 1024
        ),
        name="comm",
    )(tok, grad, weight, left_param, right_param)


def final_kernel(
    wh, wl, nl_v, nr, out, nlo, nro, nr_v, acc, S, A, sh, sl, ah, al, bh, bl, ch, cl, rh, rl, sem
):
    def copy(src, dst, index):
        made = pltpu.make_async_copy(src, dst, sem.at[index])
        made.start()
        return made

    right_in = copy(nr, nr_v, 1)
    outs = [copy(nl_v, nlo, 0)]
    param = nl_v[...]
    s = (0.5 / math.sqrt(LB)) * (param - param.T)
    S[...] = s
    put((sh, sl), s)
    poly(
        LB, 256, S, (sh, sl), (ah, al), (bh, bl), (ch, cl), A, lambda rows, value: put((rh, rl), value, rows)
    )
    right_in.wait()
    outs.append(copy(nr_v, nro, 6))
    for index in range(4):
        cols = pl.ds(256 * index, 256)
        acc[:, cols] = dot3((rh[...], rl[...]), (wh[:, cols], wl[:, cols]))
        outs.append(copy(acc.at[:, cols], out.at[:, cols], 2 + index))
    for made in outs:
        made.wait()


def final_call(wrh, wrl, new_left, new_right):
    vm = pltpu.VMEM
    hbm = pl.BlockSpec(memory_space=pltpu.HBM)
    vmem = pl.BlockSpec(memory_space=pltpu.VMEM)
    left = (LB, LB)
    return pl.pallas_call(
        final_kernel,
        out_shape=(
            jax.ShapeDtypeStruct(wrh.shape, f32), jax.ShapeDtypeStruct(left, f32),
            jax.ShapeDtypeStruct((4, RB, RB), f32),
        ),
        in_specs=[vmem, vmem, vmem, hbm],
        out_specs=(hbm,) * 3,
        scratch_shapes=[
            vm((4, RB, RB), f32), vm(wrh.shape, f32), vm(left, f32), vm(left, f32),
            *pair_of(left), *pair_of(left), *pair_of(left), *pair_of(left), *pair_of(left),
            pltpu.SemaphoreType.DMA((7,)),
        ],
        compiler_params=pltpu.CompilerParams(vmem_limit_bytes=24 * 1024 * 1024),
        name="final",
    )(wrh, wrl, new_left, new_right)


def body(tokens, grad_out, base_weight, left_param, right_param):
    left = left_param.reshape(LB, LB)
    tokens = pltpu.with_memory_space_constraint(tokens, pltpu.HBM)
    grad_out = pltpu.with_memory_space_constraint(grad_out, pltpu.HBM)
    given = comm_call(tokens, grad_out, base_weight, left, right_param)
    wrh, wrl, new_left, new_right = given
    new_right = pltpu.with_memory_space_constraint(new_right, pltpu.HBM)
    rotated, new_left, new_right = final_call(wrh, wrl, new_left, new_right)
    return rotated, new_left.reshape(1, LB, LB), new_right


def solution(mesh):
    return jax.shard_map(
        body,
        mesh=mesh,
        in_specs=(
            P("col", "row"),
            P("row", "col"),
            P("row", "col"),
            P("row", None, None),
            P("col", None, None),
        ),
        out_specs=(P("row", "col"), P("row", None, None), P("col", None, None)),
        check_vma=False,
    )
```

```python
import math

import jax
import jax.numpy as jnp
from jax import lax
from jax.experimental import pallas as pl
from jax.experimental.pallas import tpu as pltpu
from jax.sharding import PartitionSpec as P

step_rate = 0.3
epsilon = 1e-06
f32 = jnp.float32
bf16 = jnp.bfloat16
C2, C3, C4, C5, C6 = 1 / 2, 1 / 6, 1 / 24, 1 / 120, 1 / 720
LB, RB = 512, 256
NN = (((1,), (0,)), ((), ()))
NT = (((1,), (1,)), ((), ()))


def split(value):
    high = value.astype(bf16)
    return high, (value - high.astype(f32)).astype(bf16)


def put(pair, value, where=Ellipsis):
    pair[0][where], pair[1][where] = split(value)


def dot(first, second, dims=NN):
    return lax.dot_general(first, second, dims, preferred_element_type=f32)


def dot3(first, second, dims=NN):
    ah, al = first
    bh, bl = second
    return dot(ah, bh, dims) + (dot(ah, bl, dims) + dot(al, bh, dims))


def get(pair, where=Ellipsis):
    return pair[0][where], pair[1][where]


def rows_loop(total, tile, fn):
    def step(index, carry):
        fn(pl.ds(pl.multiple_of(index * tile, tile), tile))
        return carry

    lax.fori_loop(0, total // tile, step, 0)


def eye(rows, size):
    r = lax.broadcasted_iota(jnp.int32, (rows.size, size), 0) + rows.start
    c = lax.broadcasted_iota(jnp.int32, (rows.size, size), 1)
    return jnp.where(r == c, 1.0, 0.0).astype(f32)


def poly(size, tile, S, SP, AP, BP, CP, Af, finish, CT=None, pause=None, early=None):
    def square(rows):
        a = dot3(get(SP, rows), get(SP))
        Af[rows] = a
        put(AP, a, rows)

    rows_loop(size, tile, square)
    if early is not None:
        early()

    def cube(rows):
        b = dot3(get(SP, rows), get(AP))
        put(BP, b, rows)
        s = S[rows]
        a = Af[rows]
        even = C3 * eye(rows, size) + C5 * a
        odd = C4 * s + C6 * b
        put(CP, even + odd, rows)
        if CT is not None:
            put(CT, even - odd, rows)

    rows_loop(size, tile, cube)
    if pause is not None:
        pause()

    def last(rows):
        finish(rows, eye(rows, size) + S[rows] + C2 * Af[rows] + dot3(get(BP, rows), get(CP)))

    rows_loop(size, tile, last)


def adjoint(size, tile, G, GP, SP, AP, BP, CT, EP, Ea, Aa, Eb):
    def first(rows):
        c_bar = -dot3(get(BP, rows), get(GP))
        b_bar = dot3(get(GP, rows), get(CT)) + C6 * c_bar
        put(EP, b_bar, rows)
        g = G[rows]
        Ea[rows] = g + C4 * c_bar
        Aa[rows] = C2 * g + C5 * c_bar

    rows_loop(size, tile, first)
    return adjoint_end(size, tile, GP, SP, AP, EP, Ea, Aa, Eb)


def adjoint_end(size, tile, GP, SP, AP, EP, Ea, Aa, Eb):
    def second(rows):
        Ea[rows] += dot3(get(EP, rows), get(AP))
        Aa[rows] -= dot3(get(SP, rows), get(EP))

    rows_loop(size, tile, second)
    a_bar = Aa[...]
    put(GP, a_bar + a_bar.T)

    def third(rows):
        Eb[rows] = Ea[rows] - dot3(get(GP, rows), get(SP))

    rows_loop(size, tile, third)
    e = Eb[...]
    return e - e.T


def updated(param, diff, size):
    p = (0.5 / math.sqrt(size)) * diff
    mean = jnp.sum(p * p) * (1.0 / (size * size))
    return param - step_rate * p / jnp.sqrt(mean + epsilon)


def comm_kernel(
    tok_hbm, grad_ref, w_hbm, lp_hbm, rp_hbm, gwh, gwl, nl_ref, nr_hbm,
    nr_ref, tok_v, w_ref, lp_ref, rp_ref,
    T, Gr, gw, mh, ml, qh, ql,
    lS, lA, lsh, lsl, lah, lal, lbh, lbl, lch, lcl, lth, ltl, lrh, lrl, lgh, lgl,
    rS, rA, rsh, rsl, rah, ral, rbh, rbl, rch, rcl, rth, rtl, rrh, rrl,
    lpart, xr, xs, Q, zr, zs, Fx,
    rpart, rc, rq, yr, ys, ro, rz, Fy,
    t_recv, t_send, g_recv, g_send, loc_sem,
    xr_sem, zr_sem, za_sem, xa_sem, l_send,
    rc_sem, yr_sem, rz_sem, ya_sem, ra_sem, rb_sem, r_send,
):
    row = lax.axis_index("row")
    col = lax.axis_index("col")
    y, z, c = row // 4, (row // 2) % 2, row % 2
    h, x = col // 4, col % 4

    def row_of(yy, zz, cc):
        return (lax.rem(yy + 4, 4) * 2 + zz) * 2 + cc

    def col_of(hh, xx):
        return lax.rem(hh + 4, 4) * 4 + lax.rem(xx + 4, 4)

    YP, YM = {"row": row_of(y + 1, z, c)}, {"row": row_of(y + 3, z, c)}
    ZZ, CC = {"row": row_of(y, 1 - z, c)}, {"row": row_of(y, z, 1 - c)}
    XP, XM = {"col": col_of(h, x + 1)}, {"col": col_of(h, x + 3)}
    HP, HM = {"col": col_of(h + 1, x)}, {"col": col_of(h + 3, x)}
    started = []

    def send(src, dst, sems, recv, dev):
        counter = sems[1]
        copy = pltpu.make_async_remote_copy(
            src_ref=src, dst_ref=dst, send_sem=sems[0].at[counter[0]], recv_sem=recv,
            device_id=dev, device_id_type=pl.DeviceIdType.MESH,
        )
        counter[0] += 1
        copy.start()
        started.append(copy)

    def arrive(dst, recv):
        pltpu.make_async_remote_copy(
            src_ref=dst, dst_ref=dst, send_sem=loc_sem.at[5], recv_sem=recv,
            device_id=CC, device_id_type=pl.DeviceIdType.MESH,
        ).wait_recv()

    ts, gs, ls, rs = (t_send, [0]), (g_send, [0]), (l_send, [0]), (r_send, [0])

    load_tok = pltpu.make_async_copy(tok_hbm, tok_v, loc_sem.at[0])
    load_tok.start()
    barrier = pltpu.get_barrier_semaphore()
    for dev in (YP, YM, ZZ, CC, XP, XM, HP, HM):
        pl.semaphore_signal(barrier, inc=1, device_id=dev, device_id_type=pl.DeviceIdType.MESH)
    pl.semaphore_wait(barrier, 8)

    def t_half(ref, half):
        return ref.at[pl.ds(256 * half, 256)]

    def g_half(ref, half):
        return ref.at[pl.ds(64 * half, 64)]

    def t_go(shard, half, dev):
        piece = t_half(T.at[shard], half)
        send(piece, piece, ts, t_recv.at[shard, half], dev)

    def t_in(shard, half):
        arrive(t_half(T.at[shard], half), t_recv.at[shard, half])

    def g_go(shard, half, dev, own=False):
        src = g_half(grad_ref if own else Gr.at[shard], half)
        send(src, g_half(Gr.at[shard], half), gs, g_recv.at[shard, half], dev)

    def g_in(shard, half):
        arrive(g_half(Gr.at[shard], half), g_recv.at[shard, half])

    for q in range(4):
        g_go(row, q, YP, True)
        g_go(row, (q + 2) % 4, YM, True)
    load_tok.wait()
    T[col] = tok_v[...].astype(f32).T.astype(bf16)
    for half in (0, 1):
        t_go(col, half, XP)
        t_go(col, 1 - half, XM)
        t_go(col, half, HP)
        t_go(col, 1 - half, HM)
    for q in (0, 2, 1):
        g_go(row, q, ZZ, True)
    for q in range(4):
        g_go(row, q, CC, True)

    loads = [
        pltpu.make_async_copy(src, dst, loc_sem.at[1 + index])
        for index, (src, dst) in enumerate(
            ((rp_hbm, rp_ref), (lp_hbm, lp_ref), (w_hbm, w_ref), (grad_ref, Gr.at[row]))
        )
    ]
    for load in loads:
        load.start()

    def t_pass(shard, half, *devs):
        t_in(shard, half)
        for dev in devs:
            t_go(shard, half, dev)

    def g_pass(shard, half, *devs):
        g_in(shard, half)
        for dev in devs:
            g_go(shard, half, dev)
        g_go(shard, half, CC)

    lSP, lAP, lBP, lCP, lCT = (lsh, lsl), (lah, lal), (lbh, lbl), (lch, lcl), (lth, ltl)
    lRP, lGP = (lrh, lrl), (lgh, lgl)
    MP, QP, GWP = (mh, ml), (qh, ql), (gwh, gwl)

    def at(pair, index):
        return tuple(ref.at[index] for ref in pair)

    rSP, rAP, rBP, rCP, rCT = (rsh, rsl), (rah, ral), (rbh, rbl), (rch, rcl), (rth, rtl)
    rRP = (rrh, rrl)

    def right_one(index, carry, source=rp_ref, other=True):
        param = source[index]
        s = (0.5 / math.sqrt(RB)) * (param - param.T)
        rS[index] = s
        put(at(rSP, index), s)
        poly(
            RB, RB, rS.at[index], at(rSP, index), at(rAP, index), at(rBP, index), at(rCP, 0), rA.at[index],
            lambda rows, value: put(at(rRP, index), value, rows), at(rCT, index) if other else None,
        )
        return carry

    def weight_right(rows):
        for index in range(4):
            cols = slice(RB * index, RB * (index + 1))
            m = dot3(split(w_ref[rows, cols]), get(at(rRP, index)))
            put(MP, m.T, (cols, rows))

    def left_weight(index, carry):
        cols = pl.ds(pl.multiple_of(index * 256, 256), 256)
        lw = dot3(get(lRP), split(w_ref[:, cols]))
        put(QP, lw.T, cols)
        return carry

    up, down, far = y + 1, y + 3, y + 2
    other = row_of(y, 1 - z, c)

    def g_up(q, zz, *devs):
        g_pass(row_of(up, zz, c), q, *devs)

    def g_down(q, zz, *devs):
        g_pass(row_of(down, zz, c), q, *devs)

    def g_far(q, zz):
        g_pass(row_of(far, zz, c), q)

    loads[0].wait()
    lax.fori_loop(0, 4, right_one, 0)
    t_pass(col_of(h, x + 3), 0, XP)
    t_pass(col_of(h, x + 1), 1, XM)
    g_down(0, z, YP)
    g_up(2, z, YM)
    loads[2].wait()
    weight_right(pl.ds(0, 256))
    g_down(1, z, YP)
    g_up(3, z, YM)
    t_pass(col_of(h + 3, x), 0, XP, XM, HP)
    t_pass(col_of(h + 1, x), 1, XM, XP, HM)
    g_go(row, 3, ZZ, True)
    weight_right(pl.ds(256, 256))
    loads[1].wait()
    param = lp_ref[...]
    s = (0.5 / math.sqrt(LB)) * (param - param.T)
    lS[...] = s
    put(lSP, s)
    g_down(2, z)
    g_up(0, z)

    def early():
        g_down(3, z)
        g_up(1, z)
        t_pass(col_of(h + 3, x + 3), 0, XP)
        t_pass(col_of(h + 1, x + 1), 1, XM)
        t_pass(col_of(h + 3, x), 1, XM, XP)
        t_pass(col_of(h + 1, x), 0, XP, XM)

    def middle():
        g_far(0, z)
        g_far(2, z)
        g_pass(other, 0, YP, YM)

    poly(LB, 256, lS, lSP, lAP, lBP, lCP, lA, lambda rows, value: put(lRP, value, rows), lCT, middle, early)
    g_far(1, z)
    g_far(3, z)
    g_pass(other, 2, YM, YP)
    lax.fori_loop(0, 4, left_weight, 0)
    g_down(0, 1 - z, YP)
    g_pass(other, 1, YP, YM)
    t_pass(col_of(h + 3, x + 1), 1, XM)
    t_pass(col_of(h + 1, x + 3), 0, XP)
    g_up(2, 1 - z, YM)
    loads[3].wait()

    def add_chunks(pieces, start=False, end=False):
        def go(rows):
            total = None if start else gw[rows]
            for k in pieces:
                part = dot(T[k, rows], Gr[k])
                total = part if total is None else total + part
            if end:
                put(GWP, total, rows)
            else:
                gw[rows] = total

        rows_loop(LB, 512, go)

    def both(yy, zz):
        return [row_of(yy, zz, 0), row_of(yy, zz, 1)]

    def partner(yy, zz):
        far = row_of(yy, zz, 1 - c)
        for q in range(4):
            g_in(far, q)

    def t_all(hh):
        for who in range(1, 4):
            for half in (0, 1):
                key = (hh, who, half)
                if key not in seen:
                    t_in(col_of(h + hh, x + who), half)

    seen = {
        (0, 3, 0), (0, 1, 1), (3, 3, 0), (1, 1, 1), (3, 1, 1), (1, 3, 0), (2, 3, 0), (2, 1, 1),
    }
    t_all(0)
    for yy in range(4):
        partner(y + yy, z)
    add_chunks(both(h, z), start=True)
    t_pass(col_of(h + 2, x), 0, XP, XM)
    t_pass(col_of(h + 2, x), 1, XM, XP)
    g_down(1, 1 - z, YP)
    t_all(3)
    t_all(1)
    add_chunks(both(h + 1, z))
    g_pass(other, 3, YM, YP)
    g_up(0, 1 - z)
    g_down(2, 1 - z)
    add_chunks(both(h + 3, z))
    t_pass(col_of(h + 2, x + 3), 0, XP)
    t_pass(col_of(h + 2, x + 1), 1, XM)
    g_up(1, 1 - z)
    g_far(0, 1 - z)
    g_far(2, 1 - z)
    g_up(3, 1 - z, YM)
    g_down(3, 1 - z)
    g_far(1, 1 - z)
    t_all(2)
    partner(y, 1 - z)
    add_chunks(both(h + 2, z) + both(y, 1 - z))
    partner(y + 1, 1 - z)
    partner(y + 3, 1 - z)
    add_chunks(both(y + 1, 1 - z) + both(y + 3, 1 - z))
    g_far(3, 1 - z)
    partner(y + 2, 1 - z)
    add_chunks(both(y + 2, 1 - z), end=True)

    def rs_open(part, me, buf, sem, snd, plus, minus):
        far = lax.rem(me + 2, 4)
        send(part(far, 0), buf.at[0], snd, sem.at[0], plus)
        send(part(far, 1), buf.at[1], snd, sem.at[1], minus)

    def rs_single(part, me, buf, sem, snd, plus, minus):
        nxt, prv = lax.rem(me + 1, 4), lax.rem(me + 3, 4)
        send(part(nxt, 1), buf.at[2], snd, sem.at[2], plus)
        send(part(prv, 0), buf.at[3], snd, sem.at[3], minus)

    def rs_mid(part, me, buf, stage, sem, snd, plus, minus):
        nxt, prv = lax.rem(me + 1, 4), lax.rem(me + 3, 4)
        arrive(buf.at[0], sem.at[0])
        stage[0] = buf[0] + part(nxt, 0)[...]
        send(stage.at[0], buf.at[4], snd, sem.at[4], plus)
        arrive(buf.at[1], sem.at[1])
        stage[1] = buf[1] + part(prv, 1)[...]
        send(stage.at[1], buf.at[5], snd, sem.at[5], minus)

    def rs_close(part, me, buf, sem):
        for index in range(2, 6):
            arrive(buf.at[index], sem.at[index])
        first = part(me, 0)[...] + (buf[3] + buf[4])
        second = part(me, 1)[...] + (buf[2] + buf[5])
        return first, second

    def ag_open(piece, me, sem, snd, plus, minus):
        for half in (0, 1):
            send(piece(me, half), piece(me, half), snd, sem.at[me, half], plus)
            send(piece(me, 1 - half), piece(me, 1 - half), snd, sem.at[me, 1 - half], minus)

    def ag_mid(piece, me, sem, snd, plus, minus):
        nxt, prv = lax.rem(me + 1, 4), lax.rem(me + 3, 4)
        arrive(piece(prv, 0), sem.at[prv, 0])
        send(piece(prv, 0), piece(prv, 0), snd, sem.at[prv, 0], plus)
        arrive(piece(nxt, 1), sem.at[nxt, 1])
        send(piece(nxt, 1), piece(nxt, 1), snd, sem.at[nxt, 1], minus)

    def ag_close(piece, me, sem):
        far, nxt, prv = lax.rem(me + 2, 4), lax.rem(me + 1, 4), lax.rem(me + 3, 4)
        for who, half in ((prv, 1), (nxt, 0), (far, 0), (far, 1)):
            arrive(piece(who, half), sem.at[who, half])

    class Left:
        def __init__(self, p):
            self.p = p
            self.part = lambda chunk, half: lpart.at[p, chunk, half]
            self.q = lambda chunk, half: Q.at[p, chunk, half]
            self.zp = lambda chunk, half: Fx.at[p, x, chunk, half]
            self.xp = lambda chunk, half: Fx.at[p, chunk, pl.ds(2 * half, 2)]

        def compute(self):
            cols = pl.ds(256 * self.p, 256)

            def go(index, carry):
                rows = pl.ds(pl.multiple_of(index * 256, 256), 256)
                value = dot3(get(GWP, rows), (mh[:, cols], ml[:, cols]))
                lpart[self.p, pl.ds(2 * index, 2)] = value.reshape(2, 2, 64, 256)
                return carry

            lax.fori_loop(0, 2, go, 0)

        def x_open(self):
            rs_open(self.part, x, xr.at[self.p], xr_sem.at[self.p], ls, XP, XM)

        def x_single(self):
            rs_single(self.part, x, xr.at[self.p], xr_sem.at[self.p], ls, XP, XM)

        def x_mid(self):
            rs_mid(self.part, x, xr.at[self.p], xs.at[self.p], xr_sem.at[self.p], ls, XP, XM)

        def z_open(self):
            p = self.p
            first, second = rs_close(self.part, x, xr.at[p], xr_sem.at[p])
            Q[p, 0:2] = first.reshape(2, 2, 16, 256)
            Q[p, 2:4] = second.reshape(2, 2, 16, 256)
            rs_open(self.q, h, zr.at[p], zr_sem.at[p], ls, HP, HM)
            rs_single(self.q, h, zr.at[p], zr_sem.at[p], ls, HP, HM)

        def z_mid(self):
            p = self.p
            rs_mid(self.q, h, zr.at[p], zs.at[p], zr_sem.at[p], ls, HP, HM)

        def za_open(self):
            p = self.p
            first, second = rs_close(self.q, h, zr.at[p], zr_sem.at[p])
            Fx[p, x, h, 0] = first
            Fx[p, x, h, 1] = second
            ag_open(self.zp, h, za_sem.at[p], ls, HP, HM)

        def za_mid(self):
            ag_mid(self.zp, h, za_sem.at[self.p], ls, HP, HM)

        def xa_open(self):
            ag_close(self.zp, h, za_sem.at[self.p])
            ag_open(self.xp, x, xa_sem.at[self.p], ls, XP, XM)

        def xa_mid(self):
            ag_mid(self.xp, x, xa_sem.at[self.p], ls, XP, XM)

        def finish(self):
            p = self.p
            ag_close(self.xp, x, xa_sem.at[p])
            value = Fx[p].reshape(LB, 256)
            cols = slice(256 * p, 256 * (p + 1))
            pair = split(value)
            lgh[...], lgl[...] = pair

            def go(index, carry):
                rows = pl.ds(pl.multiple_of(index * 256, 256), 256)
                lA[rows, cols] = -dot3(get(lBP, rows), get(lGP))
                part = dot3(get(lGP, rows), get(lCT, cols))
                lw[rows] = part if p == 0 else lw[rows] + part
                return carry

            lax.fori_loop(0, 2, go, 0)

    def r_part(chunk, half):
        return rq.at[half, chunk]

    def y_piece(chunk, half):
        return Fy.at[chunk, half]

    lw = gw.at[:, LB : 2 * LB]
    L0, L1 = Left(0), Left(1)

    def right_partial(index):
        cols = pl.ds(pl.multiple_of(index * RB, RB), RB)
        value = dot3(get(QP, cols), (gwh[:, cols], gwl[:, cols]))
        rpart[index // 2, index % 2] = value.reshape(4, 64, RB)

    L0.compute()
    L0.x_open()
    L1.compute()
    L1.x_open()
    L0.x_single()
    right_partial(2 * (1 - c))
    right_partial(2 * (1 - c) + 1)
    send(rpart.at[1 - c], rc, rs, rc_sem.at[0], CC)
    right_partial(2 * c)
    right_partial(2 * c + 1)
    L0.x_mid()
    L1.x_single()
    arrive(rc, rc_sem.at[0])
    rq[...] = rpart[c] + rc[...]
    rs_open(r_part, y, yr, yr_sem, rs, YP, YM)
    rs_single(r_part, y, yr, yr_sem, rs, YP, YM)
    L1.x_mid()
    L0.z_open()
    rs_mid(r_part, y, yr, ys, yr_sem, rs, YP, YM)
    L1.z_open()
    L0.z_mid()
    first, second = rs_close(r_part, y, yr, yr_sem)
    ro[0] = first
    ro[1] = second
    send(ro, rz, rs, rz_sem.at[0], ZZ)
    L1.z_mid()
    L0.za_open()
    L1.za_open()
    arrive(rz, rz_sem.at[0])
    Fy[y] = ro[...] + rz[...]
    ag_open(y_piece, y, ya_sem, rs, YP, YM)
    L0.za_mid()
    L1.za_mid()
    ag_mid(y_piece, y, ya_sem, rs, YP, YM)
    L0.xa_open()
    L1.xa_open()
    ag_close(y_piece, y, ya_sem)

    def right_new(zz):
        mine = 2 * c + zz
        rS[5] = Fy[:, zz].reshape(RB, RB)
        put(at(rSP, 4), rS[5])
        diff = adjoint(
            RB, RB, rS.at[5], at(rSP, 4), at(rSP, mine), at(rAP, mine), at(rBP, mine), at(rCT, mine),
            at(rAP, 4), rA.at[4], rA.at[5], rS.at[4],
        )
        nr_ref[mine] = updated(rp_ref[mine], diff, RB)
        send(nr_ref.at[mine], nr_ref.at[mine], rs, ra_sem.at[mine], CC)

    def new_rotation(zz):
        mine = 2 * c + zz
        right_one(mine, 0, nr_ref, False)
        send(rrh.at[mine], rrh.at[mine], rs, rb_sem.at[mine, 0], CC)
        send(rrl.at[mine], rrl.at[mine], rs, rb_sem.at[mine, 1], CC)

    def turn_right(index):
        cols = pl.ds(pl.multiple_of(index * RB, RB), RB)

        def go(rows):
            gwh[rows, cols], gwl[rows, cols] = split(dot3(split(w_ref[rows, cols]), get(at(rRP, index))))

        rows_loop(LB, 512, go)

    def turn_other(zz):
        index = 2 * (1 - c) + zz
        arrive(rrh.at[index], rb_sem.at[index, 0])
        arrive(rrl.at[index], rb_sem.at[index, 1])
        turn_right(index)

    right_new(0)
    L0.xa_mid()
    right_new(1)
    new_rotation(0)
    new_rotation(1)
    L1.xa_mid()
    turn_right(2 * c)
    turn_right(2 * c + 1)
    L0.finish()
    turn_other(0)
    turn_other(1)
    for zz in (0, 1):
        arrive(nr_ref.at[2 * (1 - c) + zz], ra_sem.at[2 * (1 - c) + zz])
    put_right = pltpu.make_async_copy(nr_ref, nr_hbm, loc_sem.at[0])
    put_right.start()
    L1.finish()

    Ea, Aa = gw.at[:, 0:LB], gw.at[:, LB : 2 * LB]

    def join(rows):
        c_bar = lA[rows]
        g = jnp.concatenate([Fx[0, pl.ds(2 * (rows.start // 256), 2)].reshape(256, 256),
                             Fx[1, pl.ds(2 * (rows.start // 256), 2)].reshape(256, 256)], axis=1)
        put(lRP, lw[rows] + C6 * c_bar, rows)
        Ea[rows] = g + C4 * c_bar
        Aa[rows] = C2 * g + C5 * c_bar

    join(pl.ds(0, 256))
    join(pl.ds(256, 256))
    diff = adjoint_end(LB, 512, lCP, lSP, lAP, lRP, Ea, Aa, lA)
    nl_ref[...] = updated(lp_ref[...], diff, LB)

    for copy in started:
        copy.wait_send()
    put_right.wait()


def pair_of(shape):
    return [pltpu.VMEM(shape, bf16)] * 2


def comm_call(tok, grad, weight, left_param, right_param):
    vm = pltpu.VMEM
    dma = pltpu.SemaphoreType.DMA
    left = (LB, LB)
    right = (6, RB, RB)
    scratch = [
        vm((4, RB, RB), f32), vm((256, 512), bf16), vm((512, 1024), f32), vm(left, f32),
        vm((4, RB, RB), f32),
        vm((16, 512, 256), bf16), vm((16, 256, 1024), bf16), vm((512, 1024), f32),
        *pair_of((1024, 512)), *pair_of((1024, 512)),
        vm(left, f32), vm(left, f32), *pair_of(left), *pair_of(left), *pair_of(left), *pair_of(left), *pair_of(left),
        *pair_of(left), *pair_of((512, 256)),
        vm(right, f32), vm(right, f32), *pair_of((5, RB, RB)), *pair_of((5, RB, RB)), *pair_of((4, RB, RB)),
        *pair_of((1, RB, RB)), *pair_of((4, RB, RB)), *pair_of((4, RB, RB)),
        vm((2, 4, 2, 64, 256), f32), vm((2, 6, 64, 256), f32), vm((2, 2, 64, 256), f32), vm((2, 4, 2, 16, 256), f32),
        vm((2, 6, 16, 256), f32), vm((2, 2, 16, 256), f32), vm((2, 4, 4, 2, 16, 256), f32),
        vm((2, 2, 4, 64, RB), f32), vm((2, 4, 64, RB), f32), vm((2, 4, 64, RB), f32), vm((6, 64, RB), f32),
        vm((2, 64, RB), f32), vm((2, 64, RB), f32), vm((2, 64, RB), f32), vm((4, 2, 64, RB), f32),
        dma((16, 2)), dma((30,)), dma((16, 4)), dma((60,)), dma((6,)),
        dma((2, 6)), dma((2, 6)), dma((2, 4, 2)), dma((2, 4, 2)), dma((48,)),
        dma((1,)), dma((6,)), dma((1,)), dma((4, 2)), dma((4,)), dma((4, 2)), dma((24,)),
    ]
    hbm = pl.BlockSpec(memory_space=pltpu.HBM)
    vmem = pl.BlockSpec(memory_space=pltpu.VMEM)
    return pl.pallas_call(
        comm_kernel,
        out_shape=(
            jax.ShapeDtypeStruct(weight.shape, bf16), jax.ShapeDtypeStruct(weight.shape, bf16),
            jax.ShapeDtypeStruct(left, f32),
            jax.ShapeDtypeStruct((4, RB, RB), f32),
        ),
        in_specs=[hbm] * 5,
        out_specs=(vmem, vmem, vmem, hbm),
        scratch_shapes=scratch,
        compiler_params=pltpu.CompilerParams(
            collective_id=1, has_side_effects=True, vmem_limit_bytes=50 * 1024 * 1024
        ),
        name="comm",
    )(tok, grad, weight, left_param, right_param)


def final_kernel(
    wh, wl, nl_v, nr, out, nlo, nro, nr_v, acc, S, A, sh, sl, ah, al, bh, bl, ch, cl, rh, rl, sem
):
    def copy(src, dst, index):
        made = pltpu.make_async_copy(src, dst, sem.at[index])
        made.start()
        return made

    right_in = copy(nr, nr_v, 1)
    outs = [copy(nl_v, nlo, 0)]
    param = nl_v[...]
    s = (0.5 / math.sqrt(LB)) * (param - param.T)
    S[...] = s
    put((sh, sl), s)
    poly(
        LB, 512, S, (sh, sl), (ah, al), (bh, bl), (ch, cl), A, lambda rows, value: put((rh, rl), value, rows)
    )
    right_in.wait()
    outs.append(copy(nr_v, nro, 6))
    for index in range(2):
        cols = pl.ds(512 * index, 512)
        acc[:, cols] = dot3((rh[...], rl[...]), (wh[:, cols], wl[:, cols]))
        outs.append(copy(acc.at[:, cols], out.at[:, cols], 2 + index))
    for made in outs:
        made.wait()


def final_call(wrh, wrl, new_left, new_right):
    vm = pltpu.VMEM
    hbm = pl.BlockSpec(memory_space=pltpu.HBM)
    vmem = pl.BlockSpec(memory_space=pltpu.VMEM)
    left = (LB, LB)
    return pl.pallas_call(
        final_kernel,
        out_shape=(
            jax.ShapeDtypeStruct(wrh.shape, f32), jax.ShapeDtypeStruct(left, f32),
            jax.ShapeDtypeStruct((4, RB, RB), f32),
        ),
        in_specs=[vmem, vmem, vmem, hbm],
        out_specs=(hbm,) * 3,
        scratch_shapes=[
            vm((4, RB, RB), f32), vm(wrh.shape, f32), vm(left, f32), vm(left, f32),
            *pair_of(left), *pair_of(left), *pair_of(left), *pair_of(left), *pair_of(left),
            pltpu.SemaphoreType.DMA((7,)),
        ],
        compiler_params=pltpu.CompilerParams(vmem_limit_bytes=24 * 1024 * 1024),
        name="final",
    )(wrh, wrl, new_left, new_right)


def body(tokens, grad_out, base_weight, left_param, right_param):
    left = left_param.reshape(LB, LB)
    tokens = pltpu.with_memory_space_constraint(tokens, pltpu.HBM)
    grad_out = pltpu.with_memory_space_constraint(grad_out, pltpu.HBM)
    given = comm_call(tokens, grad_out, base_weight, left, right_param)
    wrh, wrl, new_left, new_right = given
    new_right = pltpu.with_memory_space_constraint(new_right, pltpu.HBM)
    rotated, new_left, new_right = final_call(wrh, wrl, new_left, new_right)
    return rotated, new_left.reshape(1, LB, LB), new_right


def solution(mesh):
    return jax.shard_map(
        body,
        mesh=mesh,
        in_specs=(
            P("col", "row"),
            P("row", "col"),
            P("row", "col"),
            P("row", None, None),
            P("col", None, None),
        ),
        out_specs=(P("row", "col"), P("row", None, None), P("col", None, None)),
        check_vma=False,
    )
```

```python
import math

import jax
import jax.numpy as jnp
from jax import lax
from jax.experimental import pallas as pl
from jax.experimental.pallas import tpu as pltpu
from jax.sharding import PartitionSpec as P

step_rate = 0.3
epsilon = 1e-06
f32 = jnp.float32
bf16 = jnp.bfloat16
C2, C3, C4, C5, C6 = 1 / 2, 1 / 6, 1 / 24, 1 / 120, 1 / 720
LB, RB = 512, 256
NN = (((1,), (0,)), ((), ()))
NT = (((1,), (1,)), ((), ()))


def split(value):
    high = value.astype(bf16)
    return high, (value - high.astype(f32)).astype(bf16)


def put(pair, value, where=Ellipsis):
    pair[0][where], pair[1][where] = split(value)


def dot(first, second, dims=NN):
    return lax.dot_general(first, second, dims, preferred_element_type=f32)


def dot3(first, second, dims=NN):
    ah, al = first
    bh, bl = second
    return dot(ah, bh, dims) + (dot(ah, bl, dims) + dot(al, bh, dims))


def get(pair, where=Ellipsis):
    return pair[0][where], pair[1][where]


def rows_loop(total, tile, fn):
    def step(index, carry):
        fn(pl.ds(pl.multiple_of(index * tile, tile), tile))
        return carry

    lax.fori_loop(0, total // tile, step, 0)


def eye(rows, size):
    r = lax.broadcasted_iota(jnp.int32, (rows.size, size), 0) + rows.start
    c = lax.broadcasted_iota(jnp.int32, (rows.size, size), 1)
    return jnp.where(r == c, 1.0, 0.0).astype(f32)


def poly(size, tile, S, SP, AP, BP, CP, Af, finish, CT=None, pause=None, early=None):
    def square(rows):
        a = dot3(get(SP, rows), get(SP))
        Af[rows] = a
        put(AP, a, rows)

    rows_loop(size, tile, square)
    if early is not None:
        early()

    def cube(rows):
        b = dot3(get(SP, rows), get(AP))
        put(BP, b, rows)
        s = S[rows]
        a = Af[rows]
        even = C3 * eye(rows, size) + C5 * a
        odd = C4 * s + C6 * b
        put(CP, even + odd, rows)
        if CT is not None:
            put(CT, even - odd, rows)

    rows_loop(size, tile, cube)
    if pause is not None:
        pause()

    def last(rows):
        finish(rows, eye(rows, size) + S[rows] + C2 * Af[rows] + dot3(get(BP, rows), get(CP)))

    rows_loop(size, tile, last)


def adjoint(size, tile, G, GP, SP, AP, BP, CT, EP, Ea, Aa, Eb):
    def first(rows):
        c_bar = -dot3(get(BP, rows), get(GP))
        b_bar = dot3(get(GP, rows), get(CT)) + C6 * c_bar
        put(EP, b_bar, rows)
        g = G[rows]
        Ea[rows] = g + C4 * c_bar
        Aa[rows] = C2 * g + C5 * c_bar

    rows_loop(size, tile, first)
    return adjoint_end(size, tile, GP, SP, AP, EP, Ea, Aa, Eb)


def adjoint_end(size, tile, GP, SP, AP, EP, Ea, Aa, Eb):
    def second(rows):
        Ea[rows] += dot3(get(EP, rows), get(AP))
        Aa[rows] -= dot3(get(SP, rows), get(EP))

    rows_loop(size, tile, second)
    a_bar = Aa[...]
    put(GP, a_bar + a_bar.T)

    def third(rows):
        Eb[rows] = Ea[rows] - dot3(get(GP, rows), get(SP))

    rows_loop(size, tile, third)
    e = Eb[...]
    return e - e.T


def updated(param, diff, size):
    p = (0.5 / math.sqrt(size)) * diff
    mean = jnp.sum(p * p) * (1.0 / (size * size))
    return param - step_rate * p / jnp.sqrt(mean + epsilon)


def comm_kernel(
    tok_hbm, grad_ref, w_hbm, lp_hbm, rp_hbm, gwh, gwl, nl_ref, nr_hbm,
    nr_ref, tok_v, w_ref, lp_ref, rp_ref,
    T, Gr, gw, mh, ml, qh, ql,
    lS, lA, lsh, lsl, lah, lal, lbh, lbl, lch, lcl, lth, ltl, lrh, lrl, lgh, lgl,
    rS, rA, rsh, rsl, rah, ral, rbh, rbl, rch, rcl, rth, rtl, rrh, rrl,
    lpart, xr, xs, Q, zr, zs, Fx,
    rpart, rc, rq, yr, ys, ro, rz, Fy,
    t_recv, t_send, g_recv, g_send, loc_sem,
    xr_sem, zr_sem, za_sem, xa_sem, l_send,
    rc_sem, yr_sem, rz_sem, ya_sem, ra_sem, rb_sem, r_send,
):
    row = lax.axis_index("row")
    col = lax.axis_index("col")
    y, z, c = row // 4, (row // 2) % 2, row % 2
    h, x = col // 4, col % 4

    def row_of(yy, zz, cc):
        return (lax.rem(yy + 4, 4) * 2 + zz) * 2 + cc

    def col_of(hh, xx):
        return lax.rem(hh + 4, 4) * 4 + lax.rem(xx + 4, 4)

    YP, YM = {"row": row_of(y + 1, z, c)}, {"row": row_of(y + 3, z, c)}
    ZZ, CC = {"row": row_of(y, 1 - z, c)}, {"row": row_of(y, z, 1 - c)}
    XP, XM = {"col": col_of(h, x + 1)}, {"col": col_of(h, x + 3)}
    HP, HM = {"col": col_of(h + 1, x)}, {"col": col_of(h + 3, x)}
    started = []

    def send(src, dst, sems, recv, dev):
        counter = sems[1]
        copy = pltpu.make_async_remote_copy(
            src_ref=src, dst_ref=dst, send_sem=sems[0].at[counter[0]], recv_sem=recv,
            device_id=dev, device_id_type=pl.DeviceIdType.MESH,
        )
        counter[0] += 1
        copy.start()
        started.append(copy)

    def arrive(dst, recv):
        pltpu.make_async_remote_copy(
            src_ref=dst, dst_ref=dst, send_sem=loc_sem.at[5], recv_sem=recv,
            device_id=CC, device_id_type=pl.DeviceIdType.MESH,
        ).wait_recv()

    ts, gs, ls, rs = (t_send, [0]), (g_send, [0]), (l_send, [0]), (r_send, [0])

    load_tok = pltpu.make_async_copy(tok_hbm, tok_v, loc_sem.at[0])
    load_tok.start()
    barrier = pltpu.get_barrier_semaphore()
    for dev in (YP, YM, ZZ, CC, XP, XM, HP, HM):
        pl.semaphore_signal(barrier, inc=1, device_id=dev, device_id_type=pl.DeviceIdType.MESH)
    pl.semaphore_wait(barrier, 8)

    def t_half(ref, half):
        return ref.at[pl.ds(256 * half, 256)]

    def g_half(ref, half):
        return ref.at[pl.ds(64 * half, 64)]

    def t_go(shard, half, dev):
        piece = t_half(T.at[shard], half)
        send(piece, piece, ts, t_recv.at[shard, half], dev)

    def t_in(shard, half):
        arrive(t_half(T.at[shard], half), t_recv.at[shard, half])

    def g_go(shard, half, dev, own=False):
        src = g_half(grad_ref if own else Gr.at[shard], half)
        send(src, g_half(Gr.at[shard], half), gs, g_recv.at[shard, half], dev)

    def g_in(shard, half):
        arrive(g_half(Gr.at[shard], half), g_recv.at[shard, half])

    for q in range(4):
        g_go(row, q, YP, True)
        g_go(row, (q + 2) % 4, YM, True)
    load_tok.wait()
    T[col] = tok_v[...].astype(f32).T.astype(bf16)
    for half in (0, 1):
        t_go(col, half, XP)
        t_go(col, 1 - half, XM)
        t_go(col, half, HP)
        t_go(col, 1 - half, HM)
    for q in (0, 2, 1):
        g_go(row, q, ZZ, True)
    for q in range(4):
        g_go(row, q, CC, True)

    loads = [
        pltpu.make_async_copy(src, dst, loc_sem.at[1 + index])
        for index, (src, dst) in enumerate(
            ((rp_hbm, rp_ref), (lp_hbm, lp_ref), (w_hbm, w_ref), (grad_ref, Gr.at[row]))
        )
    ]
    for load in loads:
        load.start()

    def t_pass(shard, half, *devs):
        t_in(shard, half)
        for dev in devs:
            t_go(shard, half, dev)

    def g_pass(shard, half, *devs):
        g_in(shard, half)
        for dev in devs:
            g_go(shard, half, dev)
        g_go(shard, half, CC)

    lSP, lAP, lBP, lCP, lCT = (lsh, lsl), (lah, lal), (lbh, lbl), (lch, lcl), (lth, ltl)
    lRP, lGP = (lrh, lrl), (lgh, lgl)
    MP, QP, GWP = (mh, ml), (qh, ql), (gwh, gwl)

    def at(pair, index):
        return tuple(ref.at[index] for ref in pair)

    rSP, rAP, rBP, rCP, rCT = (rsh, rsl), (rah, ral), (rbh, rbl), (rch, rcl), (rth, rtl)
    rRP = (rrh, rrl)

    def right_one(index, carry, source=rp_ref, other=True):
        param = source[index]
        s = (0.5 / math.sqrt(RB)) * (param - param.T)
        rS[index] = s
        put(at(rSP, index), s)
        poly(
            RB, RB, rS.at[index], at(rSP, index), at(rAP, index), at(rBP, index), at(rCP, 0), rA.at[index],
            lambda rows, value: put(at(rRP, index), value, rows), at(rCT, index) if other else None,
        )
        return carry

    def weight_right(rows):
        for index in range(4):
            cols = slice(RB * index, RB * (index + 1))
            m = dot3(split(w_ref[rows, cols]), get(at(rRP, index)))
            put(MP, m.T, (cols, rows))

    def left_weight(index, carry):
        cols = pl.ds(pl.multiple_of(index * 256, 256), 256)
        lw = dot3(get(lRP), split(w_ref[:, cols]))
        put(QP, lw.T, cols)
        return carry

    up, down, far = y + 1, y + 3, y + 2
    other = row_of(y, 1 - z, c)

    def g_up(q, zz, *devs):
        g_pass(row_of(up, zz, c), q, *devs)

    def g_down(q, zz, *devs):
        g_pass(row_of(down, zz, c), q, *devs)

    def g_far(q, zz):
        g_pass(row_of(far, zz, c), q)

    loads[0].wait()
    lax.fori_loop(0, 4, right_one, 0)
    t_pass(col_of(h, x + 3), 0, XP)
    t_pass(col_of(h, x + 1), 1, XM)
    g_down(0, z, YP)
    g_up(2, z, YM)
    loads[2].wait()
    weight_right(pl.ds(0, 256))
    g_down(1, z, YP)
    g_up(3, z, YM)
    t_pass(col_of(h + 3, x), 0, XP, XM, HP)
    t_pass(col_of(h + 1, x), 1, XM, XP, HM)
    g_go(row, 3, ZZ, True)
    weight_right(pl.ds(256, 256))
    loads[1].wait()
    param = lp_ref[...]
    s = (0.5 / math.sqrt(LB)) * (param - param.T)
    lS[...] = s
    put(lSP, s)
    g_down(2, z)
    g_up(0, z)

    def early():
        g_down(3, z)
        g_up(1, z)
        t_pass(col_of(h + 3, x + 3), 0, XP)
        t_pass(col_of(h + 1, x + 1), 1, XM)
        t_pass(col_of(h + 3, x), 1, XM, XP)
        t_pass(col_of(h + 1, x), 0, XP, XM)

    def middle():
        g_far(0, z)
        g_far(2, z)
        g_pass(other, 0, YP, YM)

    poly(LB, 512, lS, lSP, lAP, lBP, lCP, lA, lambda rows, value: put(lRP, value, rows), lCT, middle, early)
    g_far(1, z)
    g_far(3, z)
    g_pass(other, 2, YM, YP)
    lax.fori_loop(0, 4, left_weight, 0)
    g_down(0, 1 - z, YP)
    g_pass(other, 1, YP, YM)
    t_pass(col_of(h + 3, x + 1), 1, XM)
    t_pass(col_of(h + 1, x + 3), 0, XP)
    g_up(2, 1 - z, YM)
    loads[3].wait()

    def add_chunks(pieces, start=False, end=False):
        def go(rows):
            total = None if start else gw[rows]
            for k in pieces:
                part = dot(T[k, rows], Gr[k])
                total = part if total is None else total + part
            if end:
                put(GWP, total, rows)
            else:
                gw[rows] = total

        rows_loop(LB, 512, go)

    def both(yy, zz):
        return [row_of(yy, zz, 0), row_of(yy, zz, 1)]

    def partner(yy, zz):
        far = row_of(yy, zz, 1 - c)
        for q in range(4):
            g_in(far, q)

    def t_all(hh):
        for who in range(1, 4):
            for half in (0, 1):
                key = (hh, who, half)
                if key not in seen:
                    t_in(col_of(h + hh, x + who), half)

    seen = {
        (0, 3, 0), (0, 1, 1), (3, 3, 0), (1, 1, 1), (3, 1, 1), (1, 3, 0), (2, 3, 0), (2, 1, 1),
    }
    t_all(0)
    for yy in range(4):
        partner(y + yy, z)
    add_chunks(both(h, z), start=True)
    t_pass(col_of(h + 2, x), 0, XP, XM)
    t_pass(col_of(h + 2, x), 1, XM, XP)
    g_down(1, 1 - z, YP)
    t_all(3)
    t_all(1)
    add_chunks(both(h + 1, z))
    g_pass(other, 3, YM, YP)
    g_up(0, 1 - z)
    g_down(2, 1 - z)
    add_chunks(both(h + 3, z))
    t_pass(col_of(h + 2, x + 3), 0, XP)
    t_pass(col_of(h + 2, x + 1), 1, XM)
    g_up(1, 1 - z)
    g_far(0, 1 - z)
    g_far(2, 1 - z)
    g_up(3, 1 - z, YM)
    g_down(3, 1 - z)
    g_far(1, 1 - z)
    t_all(2)
    partner(y, 1 - z)
    add_chunks(both(h + 2, z) + both(y, 1 - z))
    partner(y + 1, 1 - z)
    partner(y + 3, 1 - z)
    add_chunks(both(y + 1, 1 - z) + both(y + 3, 1 - z))
    g_far(3, 1 - z)
    partner(y + 2, 1 - z)
    add_chunks(both(y + 2, 1 - z), end=True)

    def rs_open(part, me, buf, sem, snd, plus, minus):
        far = lax.rem(me + 2, 4)
        send(part(far, 0), buf.at[0], snd, sem.at[0], plus)
        send(part(far, 1), buf.at[1], snd, sem.at[1], minus)

    def rs_single(part, me, buf, sem, snd, plus, minus):
        nxt, prv = lax.rem(me + 1, 4), lax.rem(me + 3, 4)
        send(part(nxt, 1), buf.at[2], snd, sem.at[2], plus)
        send(part(prv, 0), buf.at[3], snd, sem.at[3], minus)

    def rs_mid(part, me, buf, stage, sem, snd, plus, minus):
        nxt, prv = lax.rem(me + 1, 4), lax.rem(me + 3, 4)
        arrive(buf.at[0], sem.at[0])
        stage[0] = buf[0] + part(nxt, 0)[...]
        send(stage.at[0], buf.at[4], snd, sem.at[4], plus)
        arrive(buf.at[1], sem.at[1])
        stage[1] = buf[1] + part(prv, 1)[...]
        send(stage.at[1], buf.at[5], snd, sem.at[5], minus)

    def rs_close(part, me, buf, sem):
        for index in range(2, 6):
            arrive(buf.at[index], sem.at[index])
        first = part(me, 0)[...] + (buf[3] + buf[4])
        second = part(me, 1)[...] + (buf[2] + buf[5])
        return first, second

    def ag_open(piece, me, sem, snd, plus, minus):
        for half in (0, 1):
            send(piece(me, half), piece(me, half), snd, sem.at[me, half], plus)
            send(piece(me, 1 - half), piece(me, 1 - half), snd, sem.at[me, 1 - half], minus)

    def ag_mid(piece, me, sem, snd, plus, minus):
        nxt, prv = lax.rem(me + 1, 4), lax.rem(me + 3, 4)
        arrive(piece(prv, 0), sem.at[prv, 0])
        send(piece(prv, 0), piece(prv, 0), snd, sem.at[prv, 0], plus)
        arrive(piece(nxt, 1), sem.at[nxt, 1])
        send(piece(nxt, 1), piece(nxt, 1), snd, sem.at[nxt, 1], minus)

    def ag_close(piece, me, sem):
        far, nxt, prv = lax.rem(me + 2, 4), lax.rem(me + 1, 4), lax.rem(me + 3, 4)
        for who, half in ((prv, 1), (nxt, 0), (far, 0), (far, 1)):
            arrive(piece(who, half), sem.at[who, half])

    class Left:
        def __init__(self, p):
            self.p = p
            self.part = lambda chunk, half: lpart.at[p, chunk, half]
            self.q = lambda chunk, half: Q.at[p, chunk, half]
            self.zp = lambda chunk, half: Fx.at[p, x, chunk, half]
            self.xp = lambda chunk, half: Fx.at[p, chunk, pl.ds(2 * half, 2)]

        def compute(self):
            cols = pl.ds(256 * self.p, 256)

            def go(index, carry):
                rows = pl.ds(pl.multiple_of(index * 256, 256), 256)
                value = dot3(get(GWP, rows), (mh[:, cols], ml[:, cols]))
                lpart[self.p, pl.ds(2 * index, 2)] = value.reshape(2, 2, 64, 256)
                return carry

            lax.fori_loop(0, 2, go, 0)

        def x_open(self):
            rs_open(self.part, x, xr.at[self.p], xr_sem.at[self.p], ls, XP, XM)

        def x_single(self):
            rs_single(self.part, x, xr.at[self.p], xr_sem.at[self.p], ls, XP, XM)

        def x_mid(self):
            rs_mid(self.part, x, xr.at[self.p], xs.at[self.p], xr_sem.at[self.p], ls, XP, XM)

        def z_open(self):
            p = self.p
            first, second = rs_close(self.part, x, xr.at[p], xr_sem.at[p])
            Q[p, 0:2] = first.reshape(2, 2, 16, 256)
            Q[p, 2:4] = second.reshape(2, 2, 16, 256)
            rs_open(self.q, h, zr.at[p], zr_sem.at[p], ls, HP, HM)
            rs_single(self.q, h, zr.at[p], zr_sem.at[p], ls, HP, HM)

        def z_mid(self):
            p = self.p
            rs_mid(self.q, h, zr.at[p], zs.at[p], zr_sem.at[p], ls, HP, HM)

        def za_open(self):
            p = self.p
            first, second = rs_close(self.q, h, zr.at[p], zr_sem.at[p])
            Fx[p, x, h, 0] = first
            Fx[p, x, h, 1] = second
            ag_open(self.zp, h, za_sem.at[p], ls, HP, HM)

        def za_mid(self):
            ag_mid(self.zp, h, za_sem.at[self.p], ls, HP, HM)

        def xa_open(self):
            ag_close(self.zp, h, za_sem.at[self.p])
            ag_open(self.xp, x, xa_sem.at[self.p], ls, XP, XM)

        def xa_mid(self):
            ag_mid(self.xp, x, xa_sem.at[self.p], ls, XP, XM)

        def finish(self):
            p = self.p
            ag_close(self.xp, x, xa_sem.at[p])
            value = Fx[p].reshape(LB, 256)
            cols = slice(256 * p, 256 * (p + 1))
            pair = split(value)
            lgh[...], lgl[...] = pair

            def go(index, carry):
                rows = pl.ds(pl.multiple_of(index * 256, 256), 256)
                lA[rows, cols] = -dot3(get(lBP, rows), get(lGP))
                part = dot3(get(lGP, rows), get(lCT, cols))
                lw[rows] = part if p == 0 else lw[rows] + part
                return carry

            lax.fori_loop(0, 2, go, 0)

    def r_part(chunk, half):
        return rq.at[half, chunk]

    def y_piece(chunk, half):
        return Fy.at[chunk, half]

    lw = gw.at[:, LB : 2 * LB]
    L0, L1 = Left(0), Left(1)

    def right_partial(index):
        cols = pl.ds(pl.multiple_of(index * RB, RB), RB)
        value = dot3(get(QP, cols), (gwh[:, cols], gwl[:, cols]))
        rpart[index // 2, index % 2] = value.reshape(4, 64, RB)

    L0.compute()
    L0.x_open()
    L1.compute()
    L1.x_open()
    L0.x_single()
    right_partial(2 * (1 - c))
    right_partial(2 * (1 - c) + 1)
    send(rpart.at[1 - c], rc, rs, rc_sem.at[0], CC)
    right_partial(2 * c)
    right_partial(2 * c + 1)
    L0.x_mid()
    L1.x_single()
    arrive(rc, rc_sem.at[0])
    rq[...] = rpart[c] + rc[...]
    rs_open(r_part, y, yr, yr_sem, rs, YP, YM)
    rs_single(r_part, y, yr, yr_sem, rs, YP, YM)
    L1.x_mid()
    L0.z_open()
    rs_mid(r_part, y, yr, ys, yr_sem, rs, YP, YM)
    L1.z_open()
    L0.z_mid()
    first, second = rs_close(r_part, y, yr, yr_sem)
    ro[0] = first
    ro[1] = second
    send(ro, rz, rs, rz_sem.at[0], ZZ)
    L1.z_mid()
    L0.za_open()
    L1.za_open()
    arrive(rz, rz_sem.at[0])
    Fy[y] = ro[...] + rz[...]
    ag_open(y_piece, y, ya_sem, rs, YP, YM)
    L0.za_mid()
    L1.za_mid()
    ag_mid(y_piece, y, ya_sem, rs, YP, YM)
    L0.xa_open()
    L1.xa_open()
    ag_close(y_piece, y, ya_sem)

    def right_new(zz):
        mine = 2 * c + zz
        rS[5] = Fy[:, zz].reshape(RB, RB)
        put(at(rSP, 4), rS[5])
        diff = adjoint(
            RB, RB, rS.at[5], at(rSP, 4), at(rSP, mine), at(rAP, mine), at(rBP, mine), at(rCT, mine),
            at(rAP, 4), rA.at[4], rA.at[5], rS.at[4],
        )
        nr_ref[mine] = updated(rp_ref[mine], diff, RB)
        send(nr_ref.at[mine], nr_ref.at[mine], rs, ra_sem.at[mine], CC)

    def new_rotation(zz):
        mine = 2 * c + zz
        right_one(mine, 0, nr_ref, False)
        send(rrh.at[mine], rrh.at[mine], rs, rb_sem.at[mine, 0], CC)
        send(rrl.at[mine], rrl.at[mine], rs, rb_sem.at[mine, 1], CC)

    def turn_right(index):
        cols = pl.ds(pl.multiple_of(index * RB, RB), RB)

        def go(rows):
            gwh[rows, cols], gwl[rows, cols] = split(dot3(split(w_ref[rows, cols]), get(at(rRP, index))))

        rows_loop(LB, 512, go)

    def turn_other(zz):
        index = 2 * (1 - c) + zz
        arrive(rrh.at[index], rb_sem.at[index, 0])
        arrive(rrl.at[index], rb_sem.at[index, 1])
        turn_right(index)

    right_new(0)
    L0.xa_mid()
    right_new(1)
    new_rotation(0)
    new_rotation(1)
    L1.xa_mid()
    turn_right(2 * c)
    turn_right(2 * c + 1)
    L0.finish()
    turn_other(0)
    turn_other(1)
    for zz in (0, 1):
        arrive(nr_ref.at[2 * (1 - c) + zz], ra_sem.at[2 * (1 - c) + zz])
    put_right = pltpu.make_async_copy(nr_ref, nr_hbm, loc_sem.at[0])
    put_right.start()
    L1.finish()

    Ea, Aa = gw.at[:, 0:LB], gw.at[:, LB : 2 * LB]

    def join(rows):
        c_bar = lA[rows]
        g = jnp.concatenate([Fx[0, pl.ds(2 * (rows.start // 256), 2)].reshape(256, 256),
                             Fx[1, pl.ds(2 * (rows.start // 256), 2)].reshape(256, 256)], axis=1)
        put(lRP, lw[rows] + C6 * c_bar, rows)
        Ea[rows] = g + C4 * c_bar
        Aa[rows] = C2 * g + C5 * c_bar

    join(pl.ds(0, 256))
    join(pl.ds(256, 256))
    diff = adjoint_end(LB, 512, lCP, lSP, lAP, lRP, Ea, Aa, lA)
    nl_ref[...] = updated(lp_ref[...], diff, LB)

    for copy in started:
        copy.wait_send()
    put_right.wait()


def pair_of(shape):
    return [pltpu.VMEM(shape, bf16)] * 2


def comm_call(tok, grad, weight, left_param, right_param):
    vm = pltpu.VMEM
    dma = pltpu.SemaphoreType.DMA
    left = (LB, LB)
    right = (6, RB, RB)
    scratch = [
        vm((4, RB, RB), f32), vm((256, 512), bf16), vm((512, 1024), f32), vm(left, f32),
        vm((4, RB, RB), f32),
        vm((16, 512, 256), bf16), vm((16, 256, 1024), bf16), vm((512, 1024), f32),
        *pair_of((1024, 512)), *pair_of((1024, 512)),
        vm(left, f32), vm(left, f32), *pair_of(left), *pair_of(left), *pair_of(left), *pair_of(left), *pair_of(left),
        *pair_of(left), *pair_of((512, 256)),
        vm(right, f32), vm(right, f32), *pair_of((5, RB, RB)), *pair_of((5, RB, RB)), *pair_of((4, RB, RB)),
        *pair_of((1, RB, RB)), *pair_of((4, RB, RB)), *pair_of((4, RB, RB)),
        vm((2, 4, 2, 64, 256), f32), vm((2, 6, 64, 256), f32), vm((2, 2, 64, 256), f32), vm((2, 4, 2, 16, 256), f32),
        vm((2, 6, 16, 256), f32), vm((2, 2, 16, 256), f32), vm((2, 4, 4, 2, 16, 256), f32),
        vm((2, 2, 4, 64, RB), f32), vm((2, 4, 64, RB), f32), vm((2, 4, 64, RB), f32), vm((6, 64, RB), f32),
        vm((2, 64, RB), f32), vm((2, 64, RB), f32), vm((2, 64, RB), f32), vm((4, 2, 64, RB), f32),
        dma((16, 2)), dma((30,)), dma((16, 4)), dma((60,)), dma((6,)),
        dma((2, 6)), dma((2, 6)), dma((2, 4, 2)), dma((2, 4, 2)), dma((48,)),
        dma((1,)), dma((6,)), dma((1,)), dma((4, 2)), dma((4,)), dma((4, 2)), dma((24,)),
    ]
    hbm = pl.BlockSpec(memory_space=pltpu.HBM)
    vmem = pl.BlockSpec(memory_space=pltpu.VMEM)
    return pl.pallas_call(
        comm_kernel,
        out_shape=(
            jax.ShapeDtypeStruct(weight.shape, bf16), jax.ShapeDtypeStruct(weight.shape, bf16),
            jax.ShapeDtypeStruct(left, f32),
            jax.ShapeDtypeStruct((4, RB, RB), f32),
        ),
        in_specs=[hbm] * 5,
        out_specs=(vmem, vmem, vmem, hbm),
        scratch_shapes=scratch,
        compiler_params=pltpu.CompilerParams(
            collective_id=1, has_side_effects=True, vmem_limit_bytes=50 * 1024 * 1024
        ),
        name="comm",
    )(tok, grad, weight, left_param, right_param)


def final_kernel(
    wh, wl, nl_v, nr, out, nlo, nro, nr_v, acc, S, A, sh, sl, ah, al, bh, bl, ch, cl, rh, rl, sem
):
    def copy(src, dst, index):
        made = pltpu.make_async_copy(src, dst, sem.at[index])
        made.start()
        return made

    right_in = copy(nr, nr_v, 1)
    outs = [copy(nl_v, nlo, 0)]
    param = nl_v[...]
    s = (0.5 / math.sqrt(LB)) * (param - param.T)
    S[...] = s
    put((sh, sl), s)
    poly(
        LB, 512, S, (sh, sl), (ah, al), (bh, bl), (ch, cl), A, lambda rows, value: put((rh, rl), value, rows)
    )
    right_in.wait()
    outs.append(copy(nr_v, nro, 6))
    for index, (start, width) in enumerate(((0, 512), (512, 256), (768, 256))):
        cols = pl.ds(start, width)
        acc[:, cols] = dot3((rh[...], rl[...]), (wh[:, cols], wl[:, cols]))
        outs.append(copy(acc.at[:, cols], out.at[:, cols], 2 + index))
    for made in outs:
        made.wait()


def final_call(wrh, wrl, new_left, new_right):
    vm = pltpu.VMEM
    hbm = pl.BlockSpec(memory_space=pltpu.HBM)
    vmem = pl.BlockSpec(memory_space=pltpu.VMEM)
    left = (LB, LB)
    return pl.pallas_call(
        final_kernel,
        out_shape=(
            jax.ShapeDtypeStruct(wrh.shape, f32), jax.ShapeDtypeStruct(left, f32),
            jax.ShapeDtypeStruct((4, RB, RB), f32),
        ),
        in_specs=[vmem, vmem, vmem, hbm],
        out_specs=(hbm,) * 3,
        scratch_shapes=[
            vm((4, RB, RB), f32), vm(wrh.shape, f32), vm(left, f32), vm(left, f32),
            *pair_of(left), *pair_of(left), *pair_of(left), *pair_of(left), *pair_of(left),
            pltpu.SemaphoreType.DMA((7,)),
        ],
        compiler_params=pltpu.CompilerParams(vmem_limit_bytes=24 * 1024 * 1024),
        name="final",
    )(wrh, wrl, new_left, new_right)


def body(tokens, grad_out, base_weight, left_param, right_param):
    left = left_param.reshape(LB, LB)
    tokens = pltpu.with_memory_space_constraint(tokens, pltpu.HBM)
    grad_out = pltpu.with_memory_space_constraint(grad_out, pltpu.HBM)
    given = comm_call(tokens, grad_out, base_weight, left, right_param)
    wrh, wrl, new_left, new_right = given
    new_right = pltpu.with_memory_space_constraint(new_right, pltpu.HBM)
    rotated, new_left, new_right = final_call(wrh, wrl, new_left, new_right)
    return rotated, new_left.reshape(1, LB, LB), new_right


def solution(mesh):
    return jax.shard_map(
        body,
        mesh=mesh,
        in_specs=(
            P("col", "row"),
            P("row", "col"),
            P("row", "col"),
            P("row", None, None),
            P("col", None, None),
        ),
        out_specs=(P("row", "col"), P("row", None, None), P("col", None, None)),
        check_vma=False,
    )
```
